128 devices in a mesh: pb: 8 (over z_hi, x), ka: 16 (over z_lo, y, core).
Axes of the slice: x: 4, y: 4, z: 4 (z_hi: 2, z_lo: 2; z = z_hi * 2 + z_lo), core: 2. Of those that a mesh axis runs over, the one named last changes fastest.
Arguments:
- feat_first: bfloat16 [32768, 128], P(('pb', 'ka')), may hold values from -16 to 16
- feat_second: bfloat16 [32768, 128], P(('ka', 'pb')), may hold values from -18 to 18
- value_weight: bfloat16 [128, 128], replicated, may hold values from -0.5 to 0.5
- out_weight: bfloat16 [128, 128], replicated, may hold values from -0.5 to 0.5
- conv_weight: bfloat16 [3, 3, 128, 128], replicated, may hold values from -0.1875 to 0.1875
- conv_bias: bfloat16 [128], replicated, may hold values from -3 to 3
Outputs:
- refined: bfloat16 [128, 256, 128], P(('pb', 'ka'))
The draws below stay inside these ranges and needn't reach their ends.
All inputs are finite; a program needn't handle non-finite values.
Results may differ from the reference program's by a relative error of at most 0.0055.
Values may be sent and summed in bfloat16 or wider, within the bound.
No kernel may reach another device: no remote copies, remote signals or barrier semaphores. Data moves between devices by JAX's collectives and lax.ppermute only.
A program may use at most 192 MiB of HBM per device.

```python
import jax
import jax.numpy as jnp
from jax import lax

C = 128
WIMG = 256
HIMG = 128
TOKENS = 32768


def draw_features(key):
    base = jax.random.fold_in(key, 7)
    key_a, key_b = jax.random.split(base, 2)
    first = 4.0 * jnp.clip(jax.random.normal(key_a, (TOKENS, C), jnp.float32), -4.0, 4.0)
    second = 3.0 * jnp.clip(jax.random.normal(key_b, (TOKENS, C), jnp.float32), -6.0, 6.0)
    return (first, second)


def draw_feat_first(key, part):
    return draw_features(key)[0].astype(jnp.bfloat16)


def draw_feat_second(key, part):
    return draw_features(key)[1].astype(jnp.bfloat16)


def bell_draw(key, extent, spread, bound, held_as=jnp.bfloat16):
    values = spread * jax.random.normal(key, extent, jnp.float32)
    return jnp.clip(values, min=-bound, max=bound).astype(held_as)


def setup_inputs(seed: int = 0) -> dict:
    arg_keys = jax.random.split(jax.random.key(seed), 7)
    feat_first = draw_feat_first(jax.random.fold_in(arg_keys[6], 71), 0)
    feat_second = draw_feat_second(jax.random.fold_in(arg_keys[6], 71), 0)
    value_weight = bell_draw(arg_keys[2], (C, C), C ** -0.5, 0.5)
    out_weight = bell_draw(arg_keys[3], (C, C), C ** -0.5, 0.5)
    conv_weight = bell_draw(arg_keys[4], (3, 3, C, C), (9 * C) ** -0.5, 0.1875)
    conv_bias = bell_draw(arg_keys[5], (C,), 0.5, 3.0)
    return dict(feat_first=feat_first, feat_second=feat_second, value_weight=value_weight, out_weight=out_weight, conv_weight=conv_weight, conv_bias=conv_bias)


def reference(feat_first, feat_second, value_weight, out_weight, conv_weight, conv_bias):
    score_scale = C ** -0.5
    values = jnp.dot(feat_second, value_weight, preferred_element_type=jnp.float32).astype(jnp.bfloat16)
    block_rows = min(512, TOKENS)
    blocks = feat_first.reshape(TOKENS // block_rows, block_rows, C)

    def attend(query_block):
        scores = jnp.dot(query_block, feat_second.T, preferred_element_type=jnp.float32) * score_scale
        row_peak = jnp.max(scores, axis=1, keepdims=True)
        expo = jnp.exp(scores - row_peak)
        row_mass = jnp.sum(expo, axis=1, keepdims=True)
        weighted = jnp.dot(expo.astype(jnp.bfloat16), values, preferred_element_type=jnp.float32)
        return (weighted / row_mass).astype(jnp.bfloat16)

    message = lax.map(attend, blocks).reshape(TOKENS, C)
    mixed_rows = (feat_first.astype(jnp.float32) + jnp.dot(message, out_weight, preferred_element_type=jnp.float32)).astype(jnp.bfloat16)
    grid_image = mixed_rows.reshape(HIMG, WIMG, C)
    padded = jnp.pad(grid_image, ((1, 1), (1, 1), (0, 0)))
    accum_sum = jnp.zeros((HIMG * WIMG, C), jnp.float32)
    for row_shift in range(3):
        for col_shift in range(3):
            window = padded[row_shift:row_shift + HIMG, col_shift:col_shift + WIMG].reshape(HIMG * WIMG, C)
            accum_sum = accum_sum + jnp.dot(window, conv_weight[row_shift, col_shift], preferred_element_type=jnp.float32)
    conv_out = accum_sum.reshape(HIMG, WIMG, C) + conv_bias.astype(jnp.float32)
    return (grid_image.astype(jnp.float32) + jax.nn.gelu(conv_out)).astype(jnp.bfloat16)
```

```python
import functools

import jax
import jax.numpy as jnp
from jax import lax
from jax.experimental import pallas as pl
from jax.experimental.pallas import tpu as pltpu
from jax.sharding import PartitionSpec as P

AXES = ("pb", "ka")
SIZES = dict(zh=2, x=4, zl=2, y=4, c=2)
LOG2E = 1.4426950408889634
VMEM = pl.BlockSpec(memory_space=pltpu.VMEM)
NT = (((1,), (1,)), ((), ()))


def place(index):
    at = {}
    for name in reversed(SIZES):
        index, at[name] = divmod(index, SIZES[name])
    at["z"] = at["zh"] * 2 + at["zl"]
    return at


def number(at):
    index = 0
    for name, size in SIZES.items():
        index = index * size + at[name]
    return index


def send(block, **shift):
    pairs = []
    for source in range(128):
        at = place(source)
        for name, step in shift.items():
            size = 4 if name == "z" else SIZES[name]
            at[name] = (at[name] + step) % size
        if "z" in shift:
            at["zh"], at["zl"] = divmod(at["z"], 2)
        pairs.append((source, number(at)))
    return lax.ppermute(block, AXES, pairs)


def params():
    return pltpu.CompilerParams(vmem_limit_bytes=48 << 20)


def attend(q, pieces, scale, start=None, chunk=512):
    peak, weighted = (None, None) if start is None else start
    ones = jnp.ones((chunk, 128), jnp.bfloat16)
    for keys_ref, values_ref in pieces:
        for at in range(0, keys_ref.shape[0], chunk):
            k = keys_ref[at : at + chunk]
            v = jnp.concatenate([values_ref[at : at + chunk], ones], axis=1)
            s = lax.dot_general(q, k, NT, preferred_element_type=jnp.float32)
            high = jnp.max(s, axis=1, keepdims=True)
            new = high if peak is None else jnp.maximum(peak, high)
            p = jnp.exp2(((s - new) * scale).astype(jnp.bfloat16))
            part = jnp.dot(p, v, preferred_element_type=jnp.float32)
            weighted = part if peak is None else weighted * jnp.exp2((peak - new) * scale) + part
            peak = new
    return peak, weighted


def project(vw, pieces, val_refs):
    out = []
    for keys_ref, val_ref in zip(pieces, val_refs):
        val_ref[...] = jnp.dot(
            keys_ref[...], vw[...], preferred_element_type=jnp.float32
        ).astype(jnp.bfloat16)
        out.append((keys_ref, val_ref))
    return out


def first_kernel(scale, nq, nk, *refs):
    q_refs, k_refs = refs[:nq], refs[nq : nq + nk]
    vw = refs[nq + nk]
    outs = refs[nq + nk + 1 : nq + nk + 1 + 2 * nq]
    vals = refs[nq + nk + 1 + 2 * nq :]
    pieces = project(vw, k_refs, vals)
    for i in range(nq):
        peak, weighted = attend(q_refs[i][...], pieces, scale)
        outs[2 * i][...] = jnp.broadcast_to(peak, (256, 128))
        outs[2 * i + 1][...] = weighted


def first_call(queries, pieces, vw, scale):
    nq, nk = len(queries), len(pieces)
    shapes = []
    for _ in range(nq):
        shapes += [
            jax.ShapeDtypeStruct((256, 128), jnp.float32),
            jax.ShapeDtypeStruct((256, 256), jnp.float32),
        ]
    out = pl.pallas_call(
        functools.partial(first_kernel, scale, nq, nk),
        out_shape=shapes,
        in_specs=[VMEM] * (nq + nk + 1),
        out_specs=[VMEM] * (2 * nq),
        scratch_shapes=[pltpu.VMEM(p.shape, jnp.bfloat16) for p in pieces],
        compiler_params=params(),
        name="first_keys",
    )(*queries, *pieces, vw)
    return [(out[2 * i], out[2 * i + 1]) for i in range(nq)]


def values_kernel(nk, *refs):
    project(refs[nk], refs[:nk], refs[nk + 1 :])


def values_call(pieces, vw):
    return pl.pallas_call(
        functools.partial(values_kernel, len(pieces)),
        out_shape=[jax.ShapeDtypeStruct(p.shape, jnp.bfloat16) for p in pieces],
        in_specs=[VMEM] * (len(pieces) + 1),
        out_specs=[VMEM] * len(pieces),
        compiler_params=params(),
        name="values",
    )(*pieces, vw)


def split3(x):
    high = x.astype(jnp.bfloat16)
    rest = x - high.astype(jnp.float32)
    mid = rest.astype(jnp.bfloat16)
    low = (rest - mid.astype(jnp.float32)).astype(jnp.bfloat16)
    return high.astype(jnp.float32), mid.astype(jnp.float32), low.astype(jnp.float32)


def pack(peak, weighted, scale, out_ref):
    mass = weighted[:, 128:]
    out_ref[0:256] = (weighted[:, :128] / mass).astype(jnp.bfloat16)
    level = peak * scale + jnp.log2(mass)
    rows = jnp.transpose(level)[0:8]
    left, right = split3(rows[:, :128]), split3(rows[:, 128:])
    at = lax.broadcasted_iota(jnp.int32, (8, 128), 0)
    tile = jnp.where(at == 0, left[0], 0.0)
    for r, part in enumerate((left[1], left[2], right[0], right[1], right[2])):
        tile = jnp.where(at == r + 1, part, tile)
    out_ref[256:272] = jnp.concatenate([tile, tile], axis=0).astype(jnp.bfloat16)


def rest_kernel(scale, nk, q_ref, peak_ref, weighted_ref, *refs):
    pieces = list(zip(refs[:nk], refs[nk : 2 * nk]))
    out_ref = refs[2 * nk]
    peak, weighted = attend(
        q_ref[...], pieces, scale, (peak_ref[:, 0:1], weighted_ref[...])
    )
    pack(peak, weighted, scale, out_ref)


def rest_call(query, state, keys, values, scale):
    nk = len(keys)
    return pl.pallas_call(
        functools.partial(rest_kernel, scale, nk),
        out_shape=jax.ShapeDtypeStruct((272, 128), jnp.bfloat16),
        in_specs=[VMEM] * (3 + 2 * nk),
        out_specs=VMEM,
        compiler_params=params(),
        name="rest_keys",
    )(query, *state, *keys, *values)


def level_row(part_ref):
    tile = part_ref[256:272].astype(jnp.float32)
    left = tile[0:1] + tile[1:2] + tile[2:3]
    right = tile[3:4] + tile[4:5] + tile[5:6]
    return jnp.concatenate([left, right], axis=1)


def merge_kernel(q_ref, ow_ref, *refs):
    parts, out_ref = refs[:-1], refs[-1]
    levels = [level_row(p) for p in parts]
    top = functools.reduce(jnp.maximum, levels)
    gains = [jnp.exp2(v - top) for v in levels]
    total = functools.reduce(jnp.add, gains)
    at = lax.broadcasted_iota(jnp.int32, (128, 256), 0)
    rows = jnp.zeros((128, 256), jnp.float32)
    for i, g in enumerate(gains):
        rows = jnp.where(at == i, g / total, rows)
    cols = jnp.transpose(rows)
    message = jnp.zeros((256, 128), jnp.float32)
    for i, p in enumerate(parts):
        message = message + p[0:256].astype(jnp.float32) * cols[:, i : i + 1]
    mixed = q_ref[...].astype(jnp.float32) + jnp.dot(
        message.astype(jnp.bfloat16), ow_ref[...], preferred_element_type=jnp.float32
    )
    out_ref[...] = mixed.astype(jnp.bfloat16)


def merge_call(query, ow, parts):
    return pl.pallas_call(
        merge_kernel,
        out_shape=jax.ShapeDtypeStruct((256, 128), jnp.bfloat16),
        in_specs=[VMEM] * (2 + len(parts)),
        out_specs=VMEM,
        compiler_params=params(),
        name="merge",
    )(query, ow, *parts)


def conv_kernel(above_ref, here_ref, below_ref, w_ref, bias_ref, out_ref):
    total = jnp.zeros((256, 384), jnp.float32)
    for a, row in enumerate((above_ref, here_ref, below_ref)):
        taps = jnp.concatenate([w_ref[a, b] for b in range(3)], axis=1)
        total = total + jnp.dot(row[...], taps, preferred_element_type=jnp.float32)
    at = lax.broadcasted_iota(jnp.int32, (256, 128), 0)
    left = jnp.where(at == 0, 0.0, pltpu.roll(total[:, 0:128], 1, 0))
    right = jnp.where(at == 255, 0.0, pltpu.roll(total[:, 256:384], 255, 0))
    conv = left + total[:, 128:256] + right + bias_ref[...].astype(jnp.float32)
    out_ref[...] = (here_ref[...].astype(jnp.float32) + jax.nn.gelu(conv)).astype(jnp.bfloat16)


def conv_call(above, here, below, w, bias):
    return pl.pallas_call(
        conv_kernel,
        out_shape=jax.ShapeDtypeStruct((256, 128), jnp.bfloat16),
        in_specs=[VMEM] * 5,
        out_specs=VMEM,
        compiler_params=params(),
        name="refine",
    )(above, here, below, w, bias.reshape(1, 128))


def local(feat_first, feat_second, value_weight, out_weight, conv_weight, conv_bias):
    scale = feat_first.shape[1] ** -0.5 * LOG2E
    near = [send(feat_second, x=s) for s in (1, 3, 2)]
    queries = [feat_first] + [send(feat_first, y=s) for s in (1, 2, 3)]
    mine = jnp.concatenate([feat_second] + near, axis=0)
    far = [send(mine, z=s) for s in (1, 3, 2)]
    other = send(mine, c=1)
    state = first_call(queries, [mine, other], value_weight, scale)
    keys = far + [send(block, c=1) for block in far]
    values = values_call(keys, value_weight)
    parts = []
    for i in (1, 2, 3, 0):
        part = rest_call(queries[i], state[i], keys, values, scale)
        parts.append(send(part, y=-i) if i else part)
    mixed = merge_call(feat_first, out_weight, parts)
    below_to_above = lax.ppermute(mixed, AXES, [(i, i + 1) for i in range(127)])
    above_to_below = lax.ppermute(mixed, AXES, [(i + 1, i) for i in range(127)])
    refined = conv_call(below_to_above, mixed, above_to_below, conv_weight, conv_bias)
    return refined.reshape(1, 256, 128)


def solution(mesh):
    in_specs = (P(("pb", "ka"), None), P(("ka", "pb"), None), P(), P(), P(), P())
    out_specs = P(("pb", "ka"), None, None)
    return jax.shard_map(local, mesh=mesh, in_specs=in_specs, out_specs=out_specs, check_vma=False)
```

```python
import functools

import jax
import jax.numpy as jnp
from jax import lax
from jax.experimental import pallas as pl
from jax.experimental.pallas import tpu as pltpu
from jax.sharding import PartitionSpec as P

AXES = ("pb", "ka")
SIZES = dict(zh=2, x=4, zl=2, y=4, c=2)
LOG2E = 1.4426950408889634
VMEM = pl.BlockSpec(memory_space=pltpu.VMEM)
NT = (((1,), (1,)), ((), ()))


def place(index):
    at = {}
    for name in reversed(SIZES):
        index, at[name] = divmod(index, SIZES[name])
    at["z"] = at["zh"] * 2 + at["zl"]
    return at


def number(at):
    index = 0
    for name, size in SIZES.items():
        index = index * size + at[name]
    return index


def moved(at, name, step):
    at = dict(at)
    size = 4 if name == "z" else SIZES[name]
    at[name] = (at[name] + step) % size
    if name == "z":
        at["zh"], at["zl"] = divmod(at["z"], 2)
    return at


def send(block, step, *names):
    pairs = []
    for source in range(128):
        at = place(source)
        pairs.append((source, number(moved(at, names[at["c"] % len(names)], step))))
    return lax.ppermute(block, AXES, pairs)


def swap(block):
    return send(block, 1, "c")


def params():
    return pltpu.CompilerParams(vmem_limit_bytes=48 << 20)


def attend(q, pieces, scale, start=None, chunk=512):
    peak, weighted = (None, None) if start is None else start
    ones = jnp.ones((chunk, 128), jnp.bfloat16)
    for keys_ref in pieces:
        for at in range(0, keys_ref.shape[0], chunk):
            k = keys_ref[at : at + chunk]
            v = jnp.concatenate([k, ones], axis=1)
            s = lax.dot_general(q, k, NT, preferred_element_type=jnp.float32)
            high = jnp.max(s, axis=1, keepdims=True)
            new = high if peak is None else jnp.maximum(peak, high)
            p = jnp.exp2(((s - new) * scale).astype(jnp.bfloat16))
            part = jnp.dot(p, v, preferred_element_type=jnp.float32)
            weighted = part if peak is None else weighted * jnp.exp2((peak - new) * scale) + part
            peak = new
    return peak, weighted


def keys_kernel(scale, nq, nk, started, *refs):
    refs = list(refs)
    take = lambda n: [refs.pop(0) for _ in range(n)]
    queries, pieces = take(nq), take(nk)
    before = take(2 * nq) if started else None
    after = refs
    for i in range(nq):
        start = (before[2 * i][:, 0:1], before[2 * i + 1][...]) if started else None
        peak, weighted = attend(queries[i][...], pieces, scale, start)
        after[2 * i][...] = jnp.broadcast_to(peak, (256, 128))
        after[2 * i + 1][...] = weighted


def cost(nq, pieces):
    scores = nq * 256 * sum(p.shape[0] for p in pieces)
    return pl.CostEstimate(flops=scores * 768, transcendentals=scores, bytes_accessed=1 << 20)


def keys_call(queries, pieces, scale, state=None):
    nq, nk = len(queries), len(pieces)
    shapes = [
        jax.ShapeDtypeStruct((256, 128), jnp.float32),
        jax.ShapeDtypeStruct((256, 256), jnp.float32),
    ] * nq
    before = [] if state is None else [part for pair in state for part in pair]
    out = pl.pallas_call(
        functools.partial(keys_kernel, scale, nq, nk, state is not None),
        out_shape=shapes,
        in_specs=[VMEM] * (nq + nk + len(before)),
        out_specs=[VMEM] * (2 * nq),
        compiler_params=params(),
        cost_estimate=cost(nq, pieces),
        name="keys",
    )(*queries, *pieces, *before)
    return [(out[2 * i], out[2 * i + 1]) for i in range(nq)]


def split3(x):
    high = x.astype(jnp.bfloat16)
    rest = x - high.astype(jnp.float32)
    mid = rest.astype(jnp.bfloat16)
    low = (rest - mid.astype(jnp.float32)).astype(jnp.bfloat16)
    return high.astype(jnp.float32), mid.astype(jnp.float32), low.astype(jnp.float32)


def pack(peak, weighted, scale, out_ref):
    mass = weighted[:, 128:]
    out_ref[0:256] = (weighted[:, :128] / mass).astype(jnp.bfloat16)
    level = peak * scale + jnp.log2(mass)
    rows = jnp.transpose(level)[0:8]
    left, right = split3(rows[:, :128]), split3(rows[:, 128:])
    at = lax.broadcasted_iota(jnp.int32, (8, 128), 0)
    tile = jnp.where(at == 0, left[0], 0.0)
    for r, part in enumerate((left[1], left[2], right[0], right[1], right[2])):
        tile = jnp.where(at == r + 1, part, tile)
    out_ref[256:272] = jnp.concatenate([tile, tile], axis=0).astype(jnp.bfloat16)


def last_kernel(scale, q_ref, peak_ref, weighted_ref, *refs):
    pieces, out_ref = refs[:-1], refs[-1]
    peak, weighted = attend(
        q_ref[...], pieces, scale, (peak_ref[:, 0:1], weighted_ref[...])
    )
    pack(peak, weighted, scale, out_ref)


def last_call(query, state, keys, scale):
    return pl.pallas_call(
        functools.partial(last_kernel, scale),
        out_shape=jax.ShapeDtypeStruct((272, 128), jnp.bfloat16),
        in_specs=[VMEM] * (3 + len(keys)),
        out_specs=VMEM,
        compiler_params=params(),
        cost_estimate=cost(1, keys),
        name="last_keys",
    )(query, *state, *keys)


def level_row(part_ref):
    tile = part_ref[256:272].astype(jnp.float32)
    left = tile[0:1] + tile[1:2] + tile[2:3]
    right = tile[3:4] + tile[4:5] + tile[5:6]
    return jnp.concatenate([left, right], axis=1)


def merge_kernel(q_ref, vw_ref, ow_ref, *refs):
    parts, out_ref = refs[:-1], refs[-1]
    levels = [level_row(p) for p in parts]
    top = functools.reduce(jnp.maximum, levels)
    gains = [jnp.exp2(v - top) for v in levels]
    total = functools.reduce(jnp.add, gains)
    at = lax.broadcasted_iota(jnp.int32, (128, 256), 0)
    rows = jnp.zeros((128, 256), jnp.float32)
    for i, g in enumerate(gains):
        rows = jnp.where(at == i, g / total, rows)
    cols = jnp.transpose(rows)
    mean = jnp.zeros((256, 128), jnp.float32)
    for i, p in enumerate(parts):
        mean = mean + p[0:256].astype(jnp.float32) * cols[:, i : i + 1]
    message = jnp.dot(mean.astype(jnp.bfloat16), vw_ref[...], preferred_element_type=jnp.float32)
    mixed = q_ref[...].astype(jnp.float32) + jnp.dot(
        message.astype(jnp.bfloat16), ow_ref[...], preferred_element_type=jnp.float32
    )
    out_ref[...] = mixed.astype(jnp.bfloat16)


def merge_call(query, vw, ow, parts):
    return pl.pallas_call(
        merge_kernel,
        out_shape=jax.ShapeDtypeStruct((256, 128), jnp.bfloat16),
        in_specs=[VMEM] * (3 + len(parts)),
        out_specs=VMEM,
        compiler_params=params(),
        name="merge",
    )(query, vw, ow, *parts)


def conv_kernel(outer_ref, here_ref, sibling_ref, w_ref, bias_ref, out_ref):
    odd = lax.axis_index("ka") % 2
    total = jnp.zeros((256, 384), jnp.float32)
    for row, a in ((outer_ref, 2 * odd), (here_ref, 1), (sibling_ref, 2 - 2 * odd)):
        taps = jnp.concatenate([w_ref[a, b] for b in range(3)], axis=1)
        total = total + jnp.dot(row[...], taps, preferred_element_type=jnp.float32)
    at = lax.broadcasted_iota(jnp.int32, (256, 128), 0)
    left = jnp.where(at == 0, 0.0, pltpu.roll(total[:, 0:128], 1, 0))
    right = jnp.where(at == 255, 0.0, pltpu.roll(total[:, 256:384], 255, 0))
    conv = left + total[:, 128:256] + right + bias_ref[...].astype(jnp.float32)
    out_ref[...] = (here_ref[...].astype(jnp.float32) + jax.nn.gelu(conv)).astype(jnp.bfloat16)


def conv_call(outer, here, sibling, w, bias):
    return pl.pallas_call(
        conv_kernel,
        out_shape=jax.ShapeDtypeStruct((256, 128), jnp.bfloat16),
        in_specs=[VMEM] * 5,
        out_specs=VMEM,
        compiler_params=params(),
        name="refine",
    )(outer, here, sibling, w, bias.reshape(1, 128))


def local(feat_first, feat_second, value_weight, out_weight, conv_weight, conv_bias):
    scale = feat_first.shape[1] ** -0.5 * LOG2E
    near = [send(feat_second, s, "x", "z") for s in (1, 3, 2)]
    queries = [feat_first] + [send(feat_first, s, "y") for s in (1, 2, 3)]
    near, queries = lax.optimization_barrier((near, queries))
    mine = jnp.concatenate([feat_second] + near, axis=0)
    far = [send(mine, s, "z", "x") for s in (1, 3, 2)]
    twin = swap(mine)
    state = keys_call(queries, [mine], scale)
    twin, state = lax.optimization_barrier((twin, state))
    state = keys_call(queries, [twin], scale, state)
    far[:2], state = lax.optimization_barrier((far[:2], state))
    twins = [swap(far[0]), swap(far[1])]
    state = keys_call(queries, far[:2], scale, state)
    far[2], twins, state = lax.optimization_barrier((far[2], twins, state))
    tail = [far[2], swap(far[2])]
    state = keys_call(queries, twins, scale, state)
    tail, state = lax.optimization_barrier((tail, state))
    parts = []
    for i in (2, 1, 3, 0):
        part = last_call(queries[i], state[i], tail, scale)
        parts.append(send(part, -i, "y") if i else part)
    mixed = merge_call(feat_first, value_weight, out_weight, parts)
    same_chip = [(i, i ^ 1) for i in range(128)]
    next_chip = [(i, i + 1) if i % 2 else (i, i - 1) for i in range(1, 127)]
    sibling = lax.ppermute(mixed, AXES, same_chip)
    outer = lax.ppermute(mixed, AXES, next_chip)
    refined = conv_call(outer, mixed, sibling, conv_weight, conv_bias)
    return refined.reshape(1, 256, 128)


def solution(mesh):
    in_specs = (P(("pb", "ka"), None), P(("ka", "pb"), None), P(), P(), P(), P())
    out_specs = P(("pb", "ka"), None, None)
    return jax.shard_map(local, mesh=mesh, in_specs=in_specs, out_specs=out_specs, check_vma=False)
```

```python
import functools

import jax
import jax.numpy as jnp
from jax import lax
from jax.experimental import pallas as pl
from jax.experimental.pallas import tpu as pltpu
from jax.sharding import PartitionSpec as P

AXES = ("pb", "ka")
SIZES = dict(zh=2, x=4, zl=2, y=4, c=2)
LOG2E = 1.4426950408889634
VMEM = pl.BlockSpec(memory_space=pltpu.VMEM)
NT = (((1,), (1,)), ((), ()))
ROWS = 128
CHUNK = 512


def place(index):
    at = {}
    for name in reversed(SIZES):
        index, at[name] = divmod(index, SIZES[name])
    at["z"] = at["zh"] * 2 + at["zl"]
    return at


def number(at):
    at = dict(at)
    at["zh"], at["zl"] = divmod(at["z"], 2)
    index = 0
    for name, size in SIZES.items():
        index = index * size + at[name]
    return index


def trade(block, kind, *names):
    pairs = []
    for source in range(128):
        at = place(source)
        name = names[at["c"] % len(names)]
        at[name] = at[name] ^ 1 if kind == "A" else 3 - at[name]
        pairs.append((source, number(at)))
    return lax.ppermute(block, AXES, pairs)


def swap(block):
    return lax.ppermute(block, AXES, [(i, i ^ 1) for i in range(128)])


def params():
    return pltpu.CompilerParams(vmem_limit_bytes=48 << 20)


def cost(rows, keys):
    scores = rows * keys
    return pl.CostEstimate(flops=scores * 768, transcendentals=scores, bytes_accessed=1 << 20)


def attend(queries, pieces, state, scale):
    ones = jnp.ones((CHUNK, 128), jnp.bfloat16)
    state = list(state)
    for keys_ref in pieces:
        for at in range(0, keys_ref.shape[0], CHUNK):
            k = keys_ref[at : at + CHUNK]
            v = jnp.concatenate([k, ones], axis=1)
            for b, q in enumerate(queries):
                s = lax.dot_general(q[...], k, NT, preferred_element_type=jnp.float32)
                new = jnp.broadcast_to(jnp.max(s, axis=1, keepdims=True), (ROWS, 128))
                if state[b] is not None:
                    new = jnp.maximum(state[b][0], new)
                all_new = jnp.concatenate([new] * (CHUNK // 128), axis=1)
                p = jnp.exp2(((s - all_new) * scale).astype(jnp.bfloat16))
                weighted = jnp.dot(p, v, preferred_element_type=jnp.float32)
                if state[b] is not None:
                    decay = jnp.exp2((state[b][0] - new) * scale)
                    weighted = state[b][1] * jnp.concatenate([decay, decay], axis=1) + weighted
                state[b] = (new, weighted)
    return state


def blocks_of(refs):
    return [ref.at[pl.ds(at, ROWS)] for ref in refs for at in range(0, ref.shape[0], ROWS)]


def keys_kernel(scale, nq, nk, started, *refs):
    refs = list(refs)
    take = lambda n: [refs.pop(0) for _ in range(n)]
    queries, pieces = blocks_of(take(nq)), take(nk)
    state = [None] * len(queries)
    if started:
        peaks, sums = blocks_of(take(1)), blocks_of(take(1))
        state = [(p[...], w[...]) for p, w in zip(peaks, sums)]
    peaks, sums = blocks_of(refs[:1]), blocks_of(refs[1:])
    for b, (peak, weighted) in enumerate(attend(queries, pieces, state, scale)):
        peaks[b][...] = peak
        sums[b][...] = weighted


def keys_call(queries, pieces, scale, state=()):
    rows = sum(q.shape[0] for q in queries)
    return pl.pallas_call(
        functools.partial(keys_kernel, scale, len(queries), len(pieces), bool(state)),
        out_shape=[
            jax.ShapeDtypeStruct((rows, 128), jnp.float32),
            jax.ShapeDtypeStruct((rows, 256), jnp.float32),
        ],
        in_specs=[VMEM] * (len(queries) + len(pieces) + len(state)),
        out_specs=[VMEM] * 2,
        compiler_params=params(),
        cost_estimate=cost(rows, sum(p.shape[0] for p in pieces)),
        name="keys",
    )(*queries, *pieces, *state)


def split3(x):
    high = x.astype(jnp.bfloat16)
    rest = x - high.astype(jnp.float32)
    mid = rest.astype(jnp.bfloat16)
    low = (rest - mid.astype(jnp.float32)).astype(jnp.bfloat16)
    return high.astype(jnp.float32), mid.astype(jnp.float32), low.astype(jnp.float32)


def pack(level, weighted, out_ref):
    mass = weighted[:, 128:]
    out_ref[0:256] = (weighted[:, :128] / mass).astype(jnp.bfloat16)
    rows = jnp.transpose(level + jnp.log2(mass))[0:8]
    left, right = split3(rows[:, :128]), split3(rows[:, 128:])
    at = lax.broadcasted_iota(jnp.int32, (8, 128), 0)
    tile = jnp.where(at == 0, left[0], 0.0)
    for r, part in enumerate((left[1], left[2], right[0], right[1], right[2])):
        tile = jnp.where(at == r + 1, part, tile)
    out_ref[256:272] = jnp.concatenate([tile, tile], axis=0).astype(jnp.bfloat16)


def absorb(level, weighted, part_ref):
    tile = part_ref[256:272].astype(jnp.float32)
    left = tile[0:1] + tile[1:2] + tile[2:3]
    right = tile[3:4] + tile[4:5] + tile[5:6]
    row = jnp.concatenate([left, right], axis=1)
    other = jnp.transpose(jnp.broadcast_to(row, (128, 256)))
    top = jnp.maximum(level, other)
    mine, theirs = jnp.exp2(level - top), jnp.exp2(other - top)
    both = part_ref[0:256].astype(jnp.float32) * theirs
    weighted = jnp.concatenate(
        [weighted[:, :128] * mine + both, weighted[:, 128:] * mine + theirs], axis=1
    )
    return top, weighted


def last_kernel(scale, row, nk, packed, *refs):
    refs = list(refs)
    q_ref, peak_ref, sum_ref = refs[:3]
    pieces, refs = refs[3 : 3 + nk], refs[3 + nk :]
    outs = refs[-1:] if packed else refs[-2:]
    arrived = refs[: len(refs) - len(outs)]
    start = row % q_ref.shape[0]
    queries = [q_ref.at[pl.ds(start + at, ROWS)] for at in range(0, 256, ROWS)]
    state = [
        (peak_ref[row + at : row + at + ROWS], sum_ref[row + at : row + at + ROWS])
        for at in range(0, 256, ROWS)
    ]
    state = attend(queries, pieces, state, scale)
    level = jnp.concatenate([peak for peak, _ in state], axis=0) * scale
    weighted = jnp.concatenate([total for _, total in state], axis=0)
    for part in arrived:
        level, weighted = absorb(level, weighted, part)
    if packed:
        pack(level, weighted, outs[0])
    else:
        outs[0][...] = level
        outs[1][...] = weighted


def last_call(query, row, state, pieces, scale, arrived=(), packed=True):
    shapes = jax.ShapeDtypeStruct((272, 128), jnp.bfloat16)
    if not packed:
        shapes = [
            jax.ShapeDtypeStruct((256, 128), jnp.float32),
            jax.ShapeDtypeStruct((256, 256), jnp.float32),
        ]
    return pl.pallas_call(
        functools.partial(last_kernel, scale, row, len(pieces), packed),
        out_shape=shapes,
        in_specs=[VMEM] * (3 + len(pieces) + len(arrived)),
        out_specs=VMEM if packed else [VMEM] * 2,
        compiler_params=params(),
        cost_estimate=cost(256, sum(p.shape[0] for p in pieces)),
        name="last_keys",
    )(query, *state, *pieces, *arrived)


def merge_kernel(q_ref, vw_ref, ow_ref, level_ref, sum_ref, *refs):
    parts, out_ref = refs[:-1], refs[-1]
    level, weighted = level_ref[...], sum_ref[...]
    for part in parts:
        level, weighted = absorb(level, weighted, part)
    mean = (weighted[:, :128] / weighted[:, 128:]).astype(jnp.bfloat16)
    message = jnp.dot(mean, vw_ref[...], preferred_element_type=jnp.float32)
    mixed = q_ref[...].astype(jnp.float32) + jnp.dot(
        message.astype(jnp.bfloat16), ow_ref[...], preferred_element_type=jnp.float32
    )
    out_ref[...] = mixed.astype(jnp.bfloat16)


def merge_call(query, vw, ow, own, parts):
    return pl.pallas_call(
        merge_kernel,
        out_shape=jax.ShapeDtypeStruct((256, 128), jnp.bfloat16),
        in_specs=[VMEM] * (5 + len(parts)),
        out_specs=VMEM,
        compiler_params=params(),
        name="merge",
    )(query, vw, ow, *own, *parts)


def conv_kernel(outer_ref, here_ref, sibling_ref, w_ref, bias_ref, out_ref):
    odd = lax.axis_index("ka") % 2
    total = jnp.zeros((256, 384), jnp.float32)
    for row, a in ((outer_ref, 2 * odd), (here_ref, 1), (sibling_ref, 2 - 2 * odd)):
        taps = jnp.concatenate([w_ref[a, b] for b in range(3)], axis=1)
        total = total + jnp.dot(row[...], taps, preferred_element_type=jnp.float32)
    at = lax.broadcasted_iota(jnp.int32, (256, 128), 0)
    left = jnp.where(at == 0, 0.0, pltpu.roll(total[:, 0:128], 1, 0))
    right = jnp.where(at == 255, 0.0, pltpu.roll(total[:, 256:384], 255, 0))
    conv = left + total[:, 128:256] + right + bias_ref[...].astype(jnp.float32)
    out_ref[...] = (here_ref[...].astype(jnp.float32) + jax.nn.gelu(conv)).astype(jnp.bfloat16)


def conv_call(outer, here, sibling, w, bias):
    return pl.pallas_call(
        conv_kernel,
        out_shape=jax.ShapeDtypeStruct((256, 128), jnp.bfloat16),
        in_specs=[VMEM] * 5,
        out_specs=VMEM,
        compiler_params=params(),
        name="refine",
    )(outer, here, sibling, w, bias.reshape(1, 128))


def local(feat_first, feat_second, value_weight, out_weight, conv_weight, conv_bias):
    scale = feat_first.shape[1] ** -0.5 * LOG2E
    fence = lax.optimization_barrier
    join = lambda *blocks: jnp.concatenate(blocks, axis=0)
    near_a = trade(feat_second, "A", "x", "z")
    query_a = trade(feat_first, "A", "y")
    near_b = trade(join(feat_second, near_a), "B", "x", "z")
    queries = [join(feat_first, query_a)]
    queries.append(trade(queries[0], "B", "y"))
    queries, near_b = fence((queries, near_b))
    mine = join(feat_second, near_a, near_b)
    far_a = trade(mine, "A", "z", "x")
    far_b = trade(mine, "B", "z", "x")
    twin = swap(mine)
    state = keys_call(queries, [mine], scale)
    twin, state = fence((twin, state))
    state = keys_call(queries, [twin], scale, state)
    far_a, far_b, state = fence((far_a, far_b, state))
    far_ab = trade(far_a, "B", "z", "x")
    twin_a, twin_b = swap(far_a), swap(far_b)
    state = keys_call(queries, [far_a, far_b], scale, state)
    far_ab, state = fence((far_ab, state))
    twin_ab = swap(far_ab)
    state = keys_call(queries, [twin_a], scale, state)
    tail = [twin_b, far_ab, twin_ab]
    tail, state = fence((tail, state))
    across = trade(last_call(queries[1], 768, state, tail, scale), "B", "y")
    from_b = trade(last_call(queries[1], 512, state, tail, scale), "B", "y")
    from_a = trade(last_call(queries[0], 256, state, tail, scale, (across,)), "A", "y")
    own = last_call(queries[0], 0, state, tail, scale, packed=False)
    mixed = merge_call(feat_first, value_weight, out_weight, own, (from_b, from_a))
    sibling = swap(mixed)
    outer = lax.ppermute(mixed, AXES, [(i, i + 1 if i % 2 else i - 1) for i in range(1, 127)])
    refined = conv_call(outer, mixed, sibling, conv_weight, conv_bias)
    return refined.reshape(1, 256, 128)


def solution(mesh):
    in_specs = (P(("pb", "ka"), None), P(("ka", "pb"), None), P(), P(), P(), P())
    out_specs = P(("pb", "ka"), None, None)
    return jax.shard_map(local, mesh=mesh, in_specs=in_specs, out_specs=out_specs, check_vma=False)
```

```python
import functools

import jax
import jax.numpy as jnp
from jax import lax
from jax.experimental import pallas as pl
from jax.experimental.pallas import tpu as pltpu
from jax.sharding import PartitionSpec as P


AXES = ("pb", "ka")
SIZES = dict(zh=2, x=4, zl=2, y=4, c=2)
LOG2E = 1.4426950408889634
VMEM = pl.BlockSpec(memory_space=pltpu.VMEM)
NT = (((1,), (1,)), ((), ()))
ROWS = 128
CHUNK = 512


def place(index):
    at = {}
    for name in reversed(SIZES):
        index, at[name] = divmod(index, SIZES[name])
    at["z"] = at["zh"] * 2 + at["zl"]
    return at


def number(at):
    at = dict(at)
    at["zh"], at["zl"] = divmod(at["z"], 2)
    index = 0
    for name, size in SIZES.items():
        index = index * size + at[name]
    return index


def trade(block, kind, *names):
    pairs = []
    for source in range(128):
        at = place(source)
        name = names[at["c"] % len(names)]
        at[name] = dict(A=at[name] ^ 1, B=3 - at[name], AB=at[name] ^ 2)[kind]
        pairs.append((source, number(at)))
    return lax.ppermute(block, AXES, pairs)


def swap(block):
    return lax.ppermute(block, AXES, [(i, i ^ 1) for i in range(128)])


def params():
    return pltpu.CompilerParams(vmem_limit_bytes=48 << 20)


def cost(rows, keys):
    scores = rows * keys
    return pl.CostEstimate(flops=scores * 768, transcendentals=scores, bytes_accessed=1 << 20)


def attend(queries, pieces, state, scale):
    ones = jnp.ones((CHUNK, 128), jnp.bfloat16)
    state = list(state)
    for keys_ref in pieces:
        for at in range(0, keys_ref.shape[0], CHUNK):
            k = keys_ref[at : at + CHUNK]
            v = jnp.concatenate([k, ones], axis=1)
            for b, q in enumerate(queries):
                s = lax.dot_general(q[...], k, NT, preferred_element_type=jnp.float32)
                new = jnp.broadcast_to(jnp.max(s, axis=1, keepdims=True), (ROWS, 128))
                if state[b] is not None:
                    new = jnp.maximum(state[b][0], new)
                all_new = jnp.concatenate([new] * (CHUNK // 128), axis=1)
                p = jnp.exp2(((s - all_new) * scale).astype(jnp.bfloat16))
                weighted = jnp.dot(p, v, preferred_element_type=jnp.float32)
                if state[b] is not None:
                    decay = jnp.exp2((state[b][0] - new) * scale)
                    weighted = state[b][1] * jnp.concatenate([decay, decay], axis=1) + weighted
                state[b] = (new, weighted)
    return state


def blocks_of(refs):
    return [ref.at[pl.ds(at, ROWS)] for ref in refs for at in range(0, ref.shape[0], ROWS)]


def keys_kernel(scale, nq, nk, started, row, *refs):
    refs = list(refs)
    take = lambda n: [refs.pop(0) for _ in range(n)]
    queries, pieces = blocks_of(take(nq)), take(nk)
    state = [None] * len(queries)
    if started:
        peaks, sums = blocks_of(take(1)), blocks_of(take(1))
        first = row // ROWS
        state = [(peaks[first + b][...], sums[first + b][...]) for b in range(len(queries))]
    peaks, sums = blocks_of(refs[:1]), blocks_of(refs[1:])
    for b, (peak, weighted) in enumerate(attend(queries, pieces, state, scale)):
        peaks[b][...] = peak
        sums[b][...] = weighted


def keys_call(queries, pieces, scale, state=(), row=0):
    rows = sum(q.shape[0] for q in queries)
    return pl.pallas_call(
        functools.partial(keys_kernel, scale, len(queries), len(pieces), bool(state), row),
        out_shape=[
            jax.ShapeDtypeStruct((rows, 128), jnp.float32),
            jax.ShapeDtypeStruct((rows, 256), jnp.float32),
        ],
        in_specs=[VMEM] * (len(queries) + len(pieces) + len(state)),
        out_specs=[VMEM] * 2,
        compiler_params=params(),
        cost_estimate=cost(rows, sum(p.shape[0] for p in pieces)),
        name="keys",
    )(*queries, *pieces, *state)


def split3(x):
    high = x.astype(jnp.bfloat16)
    rest = x - high.astype(jnp.float32)
    mid = rest.astype(jnp.bfloat16)
    low = (rest - mid.astype(jnp.float32)).astype(jnp.bfloat16)
    return high.astype(jnp.float32), mid.astype(jnp.float32), low.astype(jnp.float32)


def pack(level, weighted, out_ref):
    mass = weighted[:, 128:]
    out_ref[0:256] = (weighted[:, :128] / mass).astype(jnp.bfloat16)
    rows = jnp.transpose(level + jnp.log2(mass))[0:8]
    left, right = split3(rows[:, :128]), split3(rows[:, 128:])
    at = lax.broadcasted_iota(jnp.int32, (8, 128), 0)
    tile = jnp.where(at == 0, left[0], 0.0)
    for r, part in enumerate((left[1], left[2], right[0], right[1], right[2])):
        tile = jnp.where(at == r + 1, part, tile)
    out_ref[256:272] = jnp.concatenate([tile, tile], axis=0).astype(jnp.bfloat16)


def absorb(level, weighted, part_ref):
    tile = part_ref[256:272].astype(jnp.float32)
    left = tile[0:1] + tile[1:2] + tile[2:3]
    right = tile[3:4] + tile[4:5] + tile[5:6]
    row = jnp.concatenate([left, right], axis=1)
    other = jnp.transpose(jnp.broadcast_to(row, (128, 256)))
    top = jnp.maximum(level, other)
    mine, theirs = jnp.exp2(level - top), jnp.exp2(other - top)
    both = part_ref[0:256].astype(jnp.float32) * theirs
    weighted = jnp.concatenate(
        [weighted[:, :128] * mine + both, weighted[:, 128:] * mine + theirs], axis=1
    )
    return top, weighted


def last_kernel(scale, row, nk, packed, *refs):
    refs = list(refs)
    q_ref, peak_ref, sum_ref = refs[:3]
    pieces, refs = refs[3 : 3 + nk], refs[3 + nk :]
    outs = refs[-1:] if packed else refs[-2:]
    arrived = refs[: len(refs) - len(outs)]
    queries = blocks_of([q_ref])
    state = [
        (peak_ref[row + at : row + at + ROWS], sum_ref[row + at : row + at + ROWS])
        for at in range(0, 256, ROWS)
    ]
    state = attend(queries, pieces, state, scale)
    level = jnp.concatenate([peak for peak, _ in state], axis=0) * scale
    weighted = jnp.concatenate([total for _, total in state], axis=0)
    for part in arrived:
        level, weighted = absorb(level, weighted, part)
    if packed:
        pack(level, weighted, outs[0])
    else:
        outs[0][...] = level
        outs[1][...] = weighted


def last_call(query, row, state, pieces, scale, arrived=(), packed=True):
    shapes = jax.ShapeDtypeStruct((272, 128), jnp.bfloat16)
    if not packed:
        shapes = [
            jax.ShapeDtypeStruct((256, 128), jnp.float32),
            jax.ShapeDtypeStruct((256, 256), jnp.float32),
        ]
    return pl.pallas_call(
        functools.partial(last_kernel, scale, row, len(pieces), packed),
        out_shape=shapes,
        in_specs=[VMEM] * (3 + len(pieces) + len(arrived)),
        out_specs=VMEM if packed else [VMEM] * 2,
        compiler_params=params(),
        cost_estimate=cost(256, sum(p.shape[0] for p in pieces)),
        name="last_keys",
    )(query, *state, *pieces, *arrived)


def merge_kernel(q_ref, vw_ref, ow_ref, level_ref, sum_ref, *refs):
    parts, out_ref = refs[:-1], refs[-1]
    level, weighted = level_ref[...], sum_ref[...]
    for part in parts:
        level, weighted = absorb(level, weighted, part)
    mean = (weighted[:, :128] / weighted[:, 128:]).astype(jnp.bfloat16)
    message = jnp.dot(mean, vw_ref[...], preferred_element_type=jnp.float32)
    mixed = q_ref[...].astype(jnp.float32) + jnp.dot(
        message.astype(jnp.bfloat16), ow_ref[...], preferred_element_type=jnp.float32
    )
    out_ref[...] = mixed.astype(jnp.bfloat16)


def merge_call(query, vw, ow, own, parts):
    return pl.pallas_call(
        merge_kernel,
        out_shape=jax.ShapeDtypeStruct((256, 128), jnp.bfloat16),
        in_specs=[VMEM] * (5 + len(parts)),
        out_specs=VMEM,
        compiler_params=params(),
        name="merge",
    )(query, vw, ow, *own, *parts)


def conv_kernel(outer_ref, here_ref, sibling_ref, w_ref, bias_ref, out_ref):
    odd = lax.axis_index("ka") % 2
    total = jnp.zeros((256, 384), jnp.float32)
    for row, a in ((outer_ref, 2 * odd), (here_ref, 1), (sibling_ref, 2 - 2 * odd)):
        taps = jnp.concatenate([w_ref[a, b] for b in range(3)], axis=1)
        total = total + jnp.dot(row[...], taps, preferred_element_type=jnp.float32)
    at = lax.broadcasted_iota(jnp.int32, (256, 128), 0)
    left = jnp.where(at == 0, 0.0, pltpu.roll(total[:, 0:128], 1, 0))
    right = jnp.where(at == 255, 0.0, pltpu.roll(total[:, 256:384], 255, 0))
    conv = left + total[:, 128:256] + right + bias_ref[...].astype(jnp.float32)
    out_ref[...] = (here_ref[...].astype(jnp.float32) + jax.nn.gelu(conv)).astype(jnp.bfloat16)


def conv_call(outer, here, sibling, w, bias):
    return pl.pallas_call(
        conv_kernel,
        out_shape=jax.ShapeDtypeStruct((256, 128), jnp.bfloat16),
        in_specs=[VMEM] * 5,
        out_specs=VMEM,
        compiler_params=params(),
        name="refine",
    )(outer, here, sibling, w, bias.reshape(1, 128))


def local(feat_first, feat_second, value_weight, out_weight, conv_weight, conv_bias):
    scale = feat_first.shape[1] ** -0.5 * LOG2E
    fence = lax.optimization_barrier
    near = [trade(feat_second, kind, "x", "z") for kind in ("AB", "A", "B")]
    queries = [trade(feat_first, kind, "y") for kind in ("AB", "A", "B")]
    mine = jnp.concatenate([feat_second] + near, axis=0)
    far_ab, far_a, far_b = [trade(mine, kind, "z", "x") for kind in ("AB", "A", "B")]
    twin = swap(mine)
    query_ab, query_a, query_b = queries
    queries = [feat_first, query_a, query_b, query_ab]
    state = keys_call(queries, [mine], scale)
    twin, state = fence((twin, state))
    state = keys_call(queries, [twin], scale, state)
    far_a, far_b, state = fence((far_a, far_b, state))
    twin_a, twin_b = swap(far_a), swap(far_b)
    other = keys_call(queries[1:], [far_a, far_b], scale, state, 256)
    far_ab, other = fence((far_ab, other))
    twin_ab = swap(far_ab)
    away = keys_call(queries[2:], [twin_a, twin_b], scale, other, 256)
    twin_ab, away = fence((twin_ab, away))
    tail = [far_ab, twin_ab]
    across = last_call(query_ab, 256, away, tail, scale)
    across = trade(across, "B", "y")
    from_b = last_call(query_b, 0, away, tail, scale)
    from_b = trade(from_b, "B", "y")
    from_a = last_call(query_a, 0, other, [twin_a, twin_b] + tail, scale, (across,))
    from_a = trade(from_a, "A", "y")
    own = last_call(
        feat_first, 0, state, [far_a, far_b, twin_a, twin_b] + tail, scale, packed=False
    )
    mixed = merge_call(feat_first, value_weight, out_weight, own, (from_b, from_a))
    sibling = swap(mixed)
    pairs = [(i, i - 2 if i % 2 else i + 2) for i in range(128)]
    outer = lax.ppermute(sibling, AXES, [p for p in pairs if 0 <= p[1] < 128])
    refined = conv_call(outer, mixed, sibling, conv_weight, conv_bias)
    return refined.reshape(1, 256, 128)


def solution(mesh):
    in_specs = (P(("pb", "ka"), None), P(("ka", "pb"), None), P(), P(), P(), P())
    out_specs = P(("pb", "ka"), None, None)
    return jax.shard_map(local, mesh=mesh, in_specs=in_specs, out_specs=out_specs, check_vma=False)
```

```python
import functools

import jax
import jax.numpy as jnp
from jax import lax
from jax.experimental import pallas as pl
from jax.experimental.pallas import tpu as pltpu
from jax.sharding import PartitionSpec as P


AXES = ("pb", "ka")
SIZES = dict(zh=2, x=4, zl=2, y=4, c=2)
LOG2E = 1.4426950408889634
VMEM = pl.BlockSpec(memory_space=pltpu.VMEM)
NT = (((1,), (1,)), ((), ()))
ROWS = 128
CHUNK = 512


def place(index):
    at = {}
    for name in reversed(SIZES):
        index, at[name] = divmod(index, SIZES[name])
    at["z"] = at["zh"] * 2 + at["zl"]
    return at


def number(at):
    at = dict(at)
    at["zh"], at["zl"] = divmod(at["z"], 2)
    index = 0
    for name, size in SIZES.items():
        index = index * size + at[name]
    return index


def trade(block, kind, *names):
    pairs = []
    for source in range(128):
        at = place(source)
        name = names[at["c"] % len(names)]
        at[name] = dict(A=at[name] ^ 1, B=3 - at[name], AB=at[name] ^ 2)[kind]
        pairs.append((source, number(at)))
    return lax.ppermute(block, AXES, pairs)


def swap(block):
    return lax.ppermute(block, AXES, [(i, i ^ 1) for i in range(128)])


def params():
    return pltpu.CompilerParams(vmem_limit_bytes=48 << 20)


def cost(rows, keys):
    scores = rows * keys
    return pl.CostEstimate(flops=scores * 768, transcendentals=scores, bytes_accessed=1 << 20)


def attend(queries, pieces, state, scale):
    ones = jnp.ones((CHUNK, 128), jnp.bfloat16)
    state = list(state)
    for keys_ref in pieces:
        for at in range(0, keys_ref.shape[0], CHUNK):
            k = keys_ref[at : at + CHUNK]
            v = jnp.concatenate([k, ones], axis=1)
            for b, q in enumerate(queries):
                s = lax.dot_general(q[...], k, NT, preferred_element_type=jnp.float32)
                new = jnp.broadcast_to(jnp.max(s, axis=1, keepdims=True), (ROWS, 128))
                if state[b] is not None:
                    new = jnp.maximum(state[b][0], new)
                all_new = jnp.concatenate([new] * (CHUNK // 128), axis=1)
                p = jnp.exp2(((s - all_new) * scale).astype(jnp.bfloat16))
                weighted = jnp.dot(p, v, preferred_element_type=jnp.float32)
                if state[b] is not None:
                    decay = jnp.exp2((state[b][0] - new) * scale)
                    weighted = state[b][1] * jnp.concatenate([decay, decay], axis=1) + weighted
                state[b] = (new, weighted)
    return state


def blocks_of(refs):
    return [ref.at[pl.ds(at, ROWS)] for ref in refs for at in range(0, ref.shape[0], ROWS)]


def keys_kernel(scale, nq, nk, started, row, *refs):
    refs = list(refs)
    take = lambda n: [refs.pop(0) for _ in range(n)]
    queries, pieces = blocks_of(take(nq)), take(nk)
    state = [None] * len(queries)
    if started:
        peaks, sums = blocks_of(take(1)), blocks_of(take(1))
        first = row // ROWS
        state = [(peaks[first + b][...], sums[first + b][...]) for b in range(len(queries))]
    peaks, sums = blocks_of(refs[:1]), blocks_of(refs[1:])
    for b, (peak, weighted) in enumerate(attend(queries, pieces, state, scale)):
        peaks[b][...] = peak
        sums[b][...] = weighted


def keys_call(queries, pieces, scale, state=(), row=0):
    rows = sum(q.shape[0] for q in queries)
    return pl.pallas_call(
        functools.partial(keys_kernel, scale, len(queries), len(pieces), bool(state), row),
        out_shape=[
            jax.ShapeDtypeStruct((rows, 128), jnp.float32),
            jax.ShapeDtypeStruct((rows, 256), jnp.float32),
        ],
        in_specs=[VMEM] * (len(queries) + len(pieces) + len(state)),
        out_specs=[VMEM] * 2,
        compiler_params=params(),
        cost_estimate=cost(rows, sum(p.shape[0] for p in pieces)),
        name="keys",
    )(*queries, *pieces, *state)


def split3(x):
    high = x.astype(jnp.bfloat16)
    rest = x - high.astype(jnp.float32)
    mid = rest.astype(jnp.bfloat16)
    low = (rest - mid.astype(jnp.float32)).astype(jnp.bfloat16)
    return high.astype(jnp.float32), mid.astype(jnp.float32), low.astype(jnp.float32)


def pack(level, weighted, out_ref):
    mass = weighted[:, 128:]
    out_ref[0:256] = (weighted[:, :128] / mass).astype(jnp.bfloat16)
    rows = jnp.transpose(level + jnp.log2(mass))[0:8]
    left, right = split3(rows[:, :128]), split3(rows[:, 128:])
    at = lax.broadcasted_iota(jnp.int32, (8, 128), 0)
    tile = jnp.where(at == 0, left[0], 0.0)
    for r, part in enumerate((left[1], left[2], right[0], right[1], right[2])):
        tile = jnp.where(at == r + 1, part, tile)
    out_ref[256:272] = jnp.concatenate([tile, tile], axis=0).astype(jnp.bfloat16)


def absorb(level, weighted, part_ref):
    tile = part_ref[256:272].astype(jnp.float32)
    left = tile[0:1] + tile[1:2] + tile[2:3]
    right = tile[3:4] + tile[4:5] + tile[5:6]
    row = jnp.concatenate([left, right], axis=1)
    other = jnp.transpose(jnp.broadcast_to(row, (128, 256)))
    top = jnp.maximum(level, other)
    mine, theirs = jnp.exp2(level - top), jnp.exp2(other - top)
    both = part_ref[0:256].astype(jnp.float32) * theirs
    weighted = jnp.concatenate(
        [weighted[:, :128] * mine + both, weighted[:, 128:] * mine + theirs], axis=1
    )
    return top, weighted


def last_kernel(scale, row, nk, packed, *refs):
    refs = list(refs)
    q_ref, peak_ref, sum_ref = refs[:3]
    pieces, refs = refs[3 : 3 + nk], refs[3 + nk :]
    outs = refs
    queries = blocks_of([q_ref])
    state = [
        (peak_ref[row + at : row + at + ROWS], sum_ref[row + at : row + at + ROWS])
        for at in range(0, 256, ROWS)
    ]
    state = attend(queries, pieces, state, scale)
    level = jnp.concatenate([peak for peak, _ in state], axis=0) * scale
    weighted = jnp.concatenate([total for _, total in state], axis=0)
    if packed:
        pack(level, weighted, outs[0])
    else:
        outs[0][...] = level
        outs[1][...] = weighted


def last_call(query, row, state, pieces, scale, packed=True):
    shapes = jax.ShapeDtypeStruct((272, 128), jnp.bfloat16)
    if not packed:
        shapes = [
            jax.ShapeDtypeStruct((256, 128), jnp.float32),
            jax.ShapeDtypeStruct((256, 256), jnp.float32),
        ]
    return pl.pallas_call(
        functools.partial(last_kernel, scale, row, len(pieces), packed),
        out_shape=shapes,
        in_specs=[VMEM] * (3 + len(pieces)),
        out_specs=VMEM if packed else [VMEM] * 2,
        compiler_params=params(),
        cost_estimate=cost(256, sum(p.shape[0] for p in pieces)),
        name="last_keys",
    )(query, *state, *pieces)


def merge_kernel(q_ref, vw_ref, ow_ref, level_ref, sum_ref, *refs):
    parts, out_ref = refs[:-1], refs[-1]
    level, weighted = level_ref[...], sum_ref[...]
    for part in parts:
        level, weighted = absorb(level, weighted, part)
    mean = (weighted[:, :128] / weighted[:, 128:]).astype(jnp.bfloat16)
    message = jnp.dot(mean, vw_ref[...], preferred_element_type=jnp.float32)
    mixed = q_ref[...].astype(jnp.float32) + jnp.dot(
        message.astype(jnp.bfloat16), ow_ref[...], preferred_element_type=jnp.float32
    )
    out_ref[...] = mixed.astype(jnp.bfloat16)


def merge_call(query, vw, ow, own, parts):
    return pl.pallas_call(
        merge_kernel,
        out_shape=jax.ShapeDtypeStruct((256, 128), jnp.bfloat16),
        in_specs=[VMEM] * (5 + len(parts)),
        out_specs=VMEM,
        compiler_params=params(),
        name="merge",
    )(query, vw, ow, *own, *parts)


def taps_of(row_ref, w_ref, a):
    taps = jnp.concatenate([w_ref[a, b] for b in range(3)], axis=1)
    return jnp.dot(row_ref[...], taps, preferred_element_type=jnp.float32)


def near_rows_kernel(here_ref, sibling_ref, w_ref, out_ref):
    odd = lax.axis_index("ka") % 2
    out_ref[...] = taps_of(here_ref, w_ref, 1) + taps_of(sibling_ref, w_ref, 2 - 2 * odd)


def refine_kernel(outer_ref, here_ref, near_ref, w_ref, bias_ref, out_ref):
    odd = lax.axis_index("ka") % 2
    total = near_ref[...] + taps_of(outer_ref, w_ref, 2 * odd)
    at = lax.broadcasted_iota(jnp.int32, (256, 128), 0)
    left = jnp.where(at == 0, 0.0, pltpu.roll(total[:, 0:128], 1, 0))
    right = jnp.where(at == 255, 0.0, pltpu.roll(total[:, 256:384], 255, 0))
    conv = left + total[:, 128:256] + right + bias_ref[...].astype(jnp.float32)
    out_ref[...] = (here_ref[...].astype(jnp.float32) + jax.nn.gelu(conv)).astype(jnp.bfloat16)


def near_rows_call(here, sibling, w):
    return pl.pallas_call(
        near_rows_kernel,
        out_shape=jax.ShapeDtypeStruct((256, 384), jnp.float32),
        in_specs=[VMEM] * 3,
        out_specs=VMEM,
        compiler_params=params(),
        name="near_rows",
    )(here, sibling, w)


def refine_call(outer, here, near, w, bias):
    return pl.pallas_call(
        refine_kernel,
        out_shape=jax.ShapeDtypeStruct((256, 128), jnp.bfloat16),
        in_specs=[VMEM] * 5,
        out_specs=VMEM,
        compiler_params=params(),
        name="refine",
    )(outer, here, near, w, bias.reshape(1, 128))


def local(feat_first, feat_second, value_weight, out_weight, conv_weight, conv_bias):
    scale = feat_first.shape[1] ** -0.5 * LOG2E
    fence = lax.optimization_barrier
    near = [trade(feat_second, kind, "x", "z") for kind in ("AB", "A", "B")]
    queries = [trade(feat_first, kind, "y") for kind in ("AB", "A", "B")]
    mine = jnp.concatenate([feat_second] + near, axis=0)
    far_a, far_b, far_ab = [trade(mine, kind, "z", "x") for kind in ("A", "B", "AB")]
    twin = swap(mine)
    query_ab, query_a, query_b = queries
    queries = [feat_first, query_a, query_b, query_ab]
    state = keys_call(queries, [mine], scale)
    twin, state = fence((twin, state))
    state = keys_call(queries, [twin], scale, state)
    far_a, far_b, state = fence((far_a, far_b, state))
    twin_a, twin_b = swap(far_a), swap(far_b)
    other = keys_call(queries[1:], [far_a, far_b], scale, state, 256)
    far_ab, other = fence((far_ab, other))
    twin_ab = swap(far_ab)
    away = keys_call(queries[2:], [twin_a, twin_b], scale, other, 256)
    twin_ab, away = fence((twin_ab, away))
    tail = [far_ab, twin_ab]
    from_ab = last_call(query_ab, 256, away, tail, scale)
    from_ab = trade(from_ab, "AB", "y")
    from_b = last_call(query_b, 0, away, tail, scale)
    from_b = trade(from_b, "B", "y")
    from_a = last_call(query_a, 0, other, [twin_a, twin_b] + tail, scale)
    from_a = trade(from_a, "A", "y")
    own = last_call(
        feat_first, 0, state, [far_a, far_b, twin_a, twin_b] + tail, scale, packed=False
    )
    mixed = merge_call(feat_first, value_weight, out_weight, own, (from_ab, from_b, from_a))
    sibling = swap(mixed)
    pairs = [(i, i - 2 if i % 2 else i + 2) for i in range(128)]
    outer = lax.ppermute(sibling, AXES, [p for p in pairs if 0 <= p[1] < 128])
    rows = near_rows_call(mixed, sibling, conv_weight)
    refined = refine_call(outer, mixed, rows, conv_weight, conv_bias)
    return refined.reshape(1, 256, 128)


def solution(mesh):
    in_specs = (P(("pb", "ka"), None), P(("ka", "pb"), None), P(), P(), P(), P())
    out_specs = P(("pb", "ka"), None, None)
    return jax.shard_map(local, mesh=mesh, in_specs=in_specs, out_specs=out_specs, check_vma=False)
```

```python
import functools

import jax
import jax.numpy as jnp
from jax import lax
from jax.experimental import pallas as pl
from jax.experimental.pallas import tpu as pltpu
from jax.sharding import PartitionSpec as P


AXES = ("pb", "ka")
SIZES = dict(zh=2, x=4, zl=2, y=4, c=2)
LOG2E = 1.4426950408889634
VMEM = pl.BlockSpec(memory_space=pltpu.VMEM)
NT = (((1,), (1,)), ((), ()))
ROWS = 128
CHUNK = 512


def place(index):
    at = {}
    for name in reversed(SIZES):
        index, at[name] = divmod(index, SIZES[name])
    at["z"] = at["zh"] * 2 + at["zl"]
    return at


def number(at):
    at = dict(at)
    at["zh"], at["zl"] = divmod(at["z"], 2)
    index = 0
    for name, size in SIZES.items():
        index = index * size + at[name]
    return index


def trade(block, kind, *names):
    pairs = []
    for source in range(128):
        at = place(source)
        name = names[at["c"] % len(names)]
        at[name] = dict(A=at[name] ^ 1, B=3 - at[name], AB=at[name] ^ 2)[kind]
        pairs.append((source, number(at)))
    return lax.ppermute(block, AXES, pairs)


def swap(block):
    return lax.ppermute(block, AXES, [(i, i ^ 1) for i in range(128)])


def params():
    return pltpu.CompilerParams(vmem_limit_bytes=48 << 20)


def cost(rows, keys):
    scores = rows * keys
    return pl.CostEstimate(flops=scores * 768, transcendentals=scores, bytes_accessed=1 << 20)


def attend(queries, pieces, state, scale):
    ones = jnp.ones((CHUNK, 128), jnp.bfloat16)
    state = list(state)
    for keys_ref in pieces:
        for at in range(0, keys_ref.shape[0], CHUNK):
            k = keys_ref[at : at + CHUNK]
            v = jnp.concatenate([k, ones], axis=1)
            for b, q in enumerate(queries):
                s = lax.dot_general(q[...], k, NT, preferred_element_type=jnp.float32)
                new = jnp.broadcast_to(jnp.max(s, axis=1, keepdims=True), (ROWS, 128))
                if state[b] is not None:
                    new = jnp.maximum(state[b][0], new)
                all_new = jnp.concatenate([new] * (CHUNK // 128), axis=1)
                p = jnp.exp2(((s - all_new) * scale).astype(jnp.bfloat16))
                weighted = jnp.dot(p, v, preferred_element_type=jnp.float32)
                if state[b] is not None:
                    decay = jnp.exp2((state[b][0] - new) * scale)
                    weighted = state[b][1] * jnp.concatenate([decay, decay], axis=1) + weighted
                state[b] = (new, weighted)
    return state


def blocks_of(refs):
    return [ref.at[pl.ds(at, ROWS)] for ref in refs for at in range(0, ref.shape[0], ROWS)]


def keys_kernel(scale, nq, nk, started, row, *refs):
    refs = list(refs)
    take = lambda n: [refs.pop(0) for _ in range(n)]
    queries, pieces = blocks_of(take(nq)), take(nk)
    state = [None] * len(queries)
    if started:
        peaks, sums = blocks_of(take(1)), blocks_of(take(1))
        first = row // ROWS
        state = [(peaks[first + b][...], sums[first + b][...]) for b in range(len(queries))]
    peaks, sums = blocks_of(refs[:1]), blocks_of(refs[1:])
    for b, (peak, weighted) in enumerate(attend(queries, pieces, state, scale)):
        peaks[b][...] = peak
        sums[b][...] = weighted


def keys_call(queries, pieces, scale, state=(), row=0):
    rows = sum(q.shape[0] for q in queries)
    return pl.pallas_call(
        functools.partial(keys_kernel, scale, len(queries), len(pieces), bool(state), row),
        out_shape=[
            jax.ShapeDtypeStruct((rows, 128), jnp.float32),
            jax.ShapeDtypeStruct((rows, 256), jnp.float32),
        ],
        in_specs=[VMEM] * (len(queries) + len(pieces) + len(state)),
        out_specs=[VMEM] * 2,
        compiler_params=params(),
        cost_estimate=cost(rows, sum(p.shape[0] for p in pieces)),
        name="keys",
    )(*queries, *pieces, *state)


def join_kernel(*refs):
    out_ref = refs[-1]
    for i, ref in enumerate(refs[:-1]):
        rows = ref.shape[0]
        out_ref[i * rows : i * rows + rows] = ref[...]


def join_call(blocks):
    rows = sum(block.shape[0] for block in blocks)
    return pl.pallas_call(
        join_kernel,
        out_shape=jax.ShapeDtypeStruct((rows, 128), blocks[0].dtype),
        in_specs=[VMEM] * len(blocks),
        out_specs=VMEM,
        compiler_params=params(),
        name="join",
    )(*blocks)


def split3(x):
    high = x.astype(jnp.bfloat16)
    rest = x - high.astype(jnp.float32)
    mid = rest.astype(jnp.bfloat16)
    low = (rest - mid.astype(jnp.float32)).astype(jnp.bfloat16)
    return high.astype(jnp.float32), mid.astype(jnp.float32), low.astype(jnp.float32)


def pack(level, weighted, out_ref):
    mass = weighted[:, 128:]
    out_ref[0:256] = (weighted[:, :128] / mass).astype(jnp.bfloat16)
    rows = jnp.transpose(level + jnp.log2(mass))[0:8]
    left, right = split3(rows[:, :128]), split3(rows[:, 128:])
    at = lax.broadcasted_iota(jnp.int32, (8, 128), 0)
    tile = jnp.where(at == 0, left[0], 0.0)
    for r, part in enumerate((left[1], left[2], right[0], right[1], right[2])):
        tile = jnp.where(at == r + 1, part, tile)
    out_ref[256:272] = jnp.concatenate([tile, tile], axis=0).astype(jnp.bfloat16)


def absorb(level, weighted, part_ref):
    tile = part_ref[256:272].astype(jnp.float32)
    left = tile[0:1] + tile[1:2] + tile[2:3]
    right = tile[3:4] + tile[4:5] + tile[5:6]
    row = jnp.concatenate([left, right], axis=1)
    other = jnp.transpose(jnp.broadcast_to(row, (128, 256)))
    top = jnp.maximum(level, other)
    mine, theirs = jnp.exp2(level - top), jnp.exp2(other - top)
    both = part_ref[0:256].astype(jnp.float32) * theirs
    weighted = jnp.concatenate(
        [weighted[:, :128] * mine + both, weighted[:, 128:] * mine + theirs], axis=1
    )
    return top, weighted


def last_kernel(scale, row, nk, packed, *refs):
    refs = list(refs)
    q_ref, peak_ref, sum_ref = refs[:3]
    pieces, refs = refs[3 : 3 + nk], refs[3 + nk :]
    outs = refs
    queries = blocks_of([q_ref])
    state = [
        (peak_ref[row + at : row + at + ROWS], sum_ref[row + at : row + at + ROWS])
        for at in range(0, 256, ROWS)
    ]
    state = attend(queries, pieces, state, scale)
    level = jnp.concatenate([peak for peak, _ in state], axis=0) * scale
    weighted = jnp.concatenate([total for _, total in state], axis=0)
    if packed:
        pack(level, weighted, outs[0])
    else:
        outs[0][...] = level
        outs[1][...] = weighted


def last_call(query, row, state, pieces, scale, packed=True):
    shapes = jax.ShapeDtypeStruct((272, 128), jnp.bfloat16)
    if not packed:
        shapes = [
            jax.ShapeDtypeStruct((256, 128), jnp.float32),
            jax.ShapeDtypeStruct((256, 256), jnp.float32),
        ]
    return pl.pallas_call(
        functools.partial(last_kernel, scale, row, len(pieces), packed),
        out_shape=shapes,
        in_specs=[VMEM] * (3 + len(pieces)),
        out_specs=VMEM if packed else [VMEM] * 2,
        compiler_params=params(),
        cost_estimate=cost(256, sum(p.shape[0] for p in pieces)),
        name="last_keys",
    )(query, *state, *pieces)


def merge_kernel(q_ref, vw_ref, ow_ref, level_ref, sum_ref, *refs):
    parts, out_ref = refs[:-1], refs[-1]
    level, weighted = level_ref[...], sum_ref[...]
    for part in parts:
        level, weighted = absorb(level, weighted, part)
    mean = (weighted[:, :128] / weighted[:, 128:]).astype(jnp.bfloat16)
    message = jnp.dot(mean, vw_ref[...], preferred_element_type=jnp.float32)
    mixed = q_ref[...].astype(jnp.float32) + jnp.dot(
        message.astype(jnp.bfloat16), ow_ref[...], preferred_element_type=jnp.float32
    )
    out_ref[...] = mixed.astype(jnp.bfloat16)


def merge_call(query, vw, ow, own, parts):
    return pl.pallas_call(
        merge_kernel,
        out_shape=jax.ShapeDtypeStruct((256, 128), jnp.bfloat16),
        in_specs=[VMEM] * (5 + len(parts)),
        out_specs=VMEM,
        compiler_params=params(),
        name="merge",
    )(query, vw, ow, *own, *parts)


def taps_of(row_ref, w_ref, a):
    taps = jnp.concatenate([w_ref[a, b] for b in range(3)], axis=1)
    return jnp.dot(row_ref[...], taps, preferred_element_type=jnp.float32)


def near_rows_kernel(here_ref, sibling_ref, w_ref, out_ref):
    odd = lax.axis_index("ka") % 2
    out_ref[...] = taps_of(here_ref, w_ref, 1) + taps_of(sibling_ref, w_ref, 2 - 2 * odd)


def refine_kernel(outer_ref, here_ref, near_ref, w_ref, bias_ref, out_ref):
    odd = lax.axis_index("ka") % 2
    total = near_ref[...] + taps_of(outer_ref, w_ref, 2 * odd)
    at = lax.broadcasted_iota(jnp.int32, (256, 128), 0)
    left = jnp.where(at == 0, 0.0, pltpu.roll(total[:, 0:128], 1, 0))
    right = jnp.where(at == 255, 0.0, pltpu.roll(total[:, 256:384], 255, 0))
    conv = left + total[:, 128:256] + right + bias_ref[...].astype(jnp.float32)
    out_ref[...] = (here_ref[...].astype(jnp.float32) + jax.nn.gelu(conv)).astype(jnp.bfloat16)


def near_rows_call(here, sibling, w):
    return pl.pallas_call(
        near_rows_kernel,
        out_shape=jax.ShapeDtypeStruct((256, 384), jnp.float32),
        in_specs=[VMEM] * 3,
        out_specs=VMEM,
        compiler_params=params(),
        name="near_rows",
    )(here, sibling, w)


def refine_call(outer, here, near, w, bias):
    return pl.pallas_call(
        refine_kernel,
        out_shape=jax.ShapeDtypeStruct((256, 128), jnp.bfloat16),
        in_specs=[VMEM] * 5,
        out_specs=VMEM,
        compiler_params=params(),
        name="refine",
    )(outer, here, near, w, bias.reshape(1, 128))


def local(feat_first, feat_second, value_weight, out_weight, conv_weight, conv_bias):
    scale = feat_first.shape[1] ** -0.5 * LOG2E
    fence = lax.optimization_barrier
    near = [trade(feat_second, kind, "x", "z") for kind in ("AB", "A", "B")]
    queries = [trade(feat_first, kind, "y") for kind in ("AB", "A", "B")]
    mine = join_call([feat_second] + near)
    far_a, far_b, far_ab = [trade(mine, kind, "z", "x") for kind in ("A", "B", "AB")]
    twin = swap(mine)
    query_ab, query_a, query_b = queries
    queries = [feat_first, query_a, query_b, query_ab]
    state = keys_call(queries, [mine], scale)
    twin, state = fence((twin, state))
    state = keys_call(queries, [twin], scale, state)
    far_a, far_b, state = fence((far_a, far_b, state))
    twin_a, twin_b = swap(far_a), swap(far_b)
    other = keys_call(queries[1:], [far_a, far_b], scale, state, 256)
    far_ab, other = fence((far_ab, other))
    twin_ab = swap(far_ab)
    away = keys_call(queries[2:], [twin_a, twin_b], scale, other, 256)
    twin_ab, away = fence((twin_ab, away))
    tail = [far_ab, twin_ab]
    from_ab = last_call(query_ab, 256, away, tail, scale)
    from_ab = trade(from_ab, "AB", "y")
    from_b = last_call(query_b, 0, away, tail, scale)
    from_b = trade(from_b, "B", "y")
    from_a = last_call(query_a, 0, other, [twin_a, twin_b] + tail, scale)
    from_a = trade(from_a, "A", "y")
    own = last_call(
        feat_first, 0, state, [far_a, far_b, twin_a, twin_b] + tail, scale, packed=False
    )
    mixed = merge_call(feat_first, value_weight, out_weight, own, (from_ab, from_b, from_a))
    outer = lax.ppermute(mixed, AXES, [(i, i + 1 if i % 2 else i - 1) for i in range(1, 127)])
    sibling = swap(mixed)
    rows = near_rows_call(mixed, sibling, conv_weight)
    refined = refine_call(outer, mixed, rows, conv_weight, conv_bias)
    return refined.reshape(1, 256, 128)


def solution(mesh):
    in_specs = (P(("pb", "ka"), None), P(("ka", "pb"), None), P(), P(), P(), P())
    out_specs = P(("pb", "ka"), None, None)
    return jax.shard_map(local, mesh=mesh, in_specs=in_specs, out_specs=out_specs, check_vma=False)
```

```python
import functools

import jax
import jax.numpy as jnp
from jax import lax
from jax.experimental import pallas as pl
from jax.experimental.pallas import tpu as pltpu
from jax.sharding import PartitionSpec as P


AXES = ("pb", "ka")
SIZES = dict(zh=2, x=4, zl=2, y=4, c=2)
LOG2E = 1.4426950408889634
VMEM = pl.BlockSpec(memory_space=pltpu.VMEM)
NT = (((1,), (1,)), ((), ()))
ROWS = 128
CHUNK = 512


def place(index):
    at = {}
    for name in reversed(SIZES):
        index, at[name] = divmod(index, SIZES[name])
    at["z"] = at["zh"] * 2 + at["zl"]
    return at


def number(at):
    at = dict(at)
    at["zh"], at["zl"] = divmod(at["z"], 2)
    index = 0
    for name, size in SIZES.items():
        index = index * size + at[name]
    return index


def trade(block, kind, *names):
    pairs = []
    for source in range(128):
        at = place(source)
        name = names[at["c"] % len(names)]
        at[name] = dict(A=at[name] ^ 1, B=3 - at[name], AB=at[name] ^ 2)[kind]
        pairs.append((source, number(at)))
    return lax.ppermute(block, AXES, pairs)


def swap(block):
    return lax.ppermute(block, AXES, [(i, i ^ 1) for i in range(128)])


def params():
    return pltpu.CompilerParams(vmem_limit_bytes=48 << 20)


def cost(rows, keys):
    scores = rows * keys
    return pl.CostEstimate(flops=scores * 768, transcendentals=scores, bytes_accessed=1 << 20)


def attend(queries, pieces, state, scale):
    ones = jnp.ones((CHUNK, 128), jnp.bfloat16)
    state = list(state)
    for keys_ref in pieces:
        for at in range(0, keys_ref.shape[0], CHUNK):
            k = keys_ref[at : at + CHUNK]
            v = jnp.concatenate([k, ones], axis=1)
            for b, q in enumerate(queries):
                s = lax.dot_general(q[...], k, NT, preferred_element_type=jnp.float32)
                new = jnp.broadcast_to(jnp.max(s, axis=1, keepdims=True), (ROWS, 128))
                if state[b] is not None:
                    new = jnp.maximum(state[b][0], new)
                all_new = jnp.concatenate([new] * (CHUNK // 128), axis=1)
                p = jnp.exp2(((s - all_new) * scale).astype(jnp.bfloat16))
                weighted = jnp.dot(p, v, preferred_element_type=jnp.float32)
                if state[b] is not None:
                    decay = jnp.exp2((state[b][0] - new) * scale)
                    weighted = state[b][1] * jnp.concatenate([decay, decay], axis=1) + weighted
                state[b] = (new, weighted)
    return state


def blocks_of(refs):
    return [ref.at[pl.ds(at, ROWS)] for ref in refs for at in range(0, ref.shape[0], ROWS)]


def keys_kernel(scale, nq, nk, started, row, *refs):
    refs = list(refs)
    take = lambda n: [refs.pop(0) for _ in range(n)]
    queries, pieces = blocks_of(take(nq)), take(nk)
    state = [None] * len(queries)
    if started:
        peaks, sums = blocks_of(take(1)), blocks_of(take(1))
        first = row // ROWS
        state = [(peaks[first + b][...], sums[first + b][...]) for b in range(len(queries))]
    peaks, sums = blocks_of(refs[:1]), blocks_of(refs[1:])
    for b, (peak, weighted) in enumerate(attend(queries, pieces, state, scale)):
        peaks[b][...] = peak
        sums[b][...] = weighted


def keys_call(queries, pieces, scale, state=(), row=0):
    rows = sum(q.shape[0] for q in queries)
    return pl.pallas_call(
        functools.partial(keys_kernel, scale, len(queries), len(pieces), bool(state), row),
        out_shape=[
            jax.ShapeDtypeStruct((rows, 128), jnp.float32),
            jax.ShapeDtypeStruct((rows, 256), jnp.float32),
        ],
        in_specs=[VMEM] * (len(queries) + len(pieces) + len(state)),
        out_specs=[VMEM] * 2,
        compiler_params=params(),
        cost_estimate=cost(rows, sum(p.shape[0] for p in pieces)),
        name="keys",
    )(*queries, *pieces, *state)


def stage_kernel(own_ref, out_ref):
    out_ref[0 : own_ref.shape[0]] = own_ref[...]


def join_kernel(staged_ref, *refs):
    out_ref = refs[-1]
    for i, ref in enumerate(refs[:-1]):
        rows = ref.shape[0]
        out_ref[(i + 1) * rows : (i + 2) * rows] = ref[...]


def stage_call(own, count):
    return pl.pallas_call(
        stage_kernel,
        out_shape=jax.ShapeDtypeStruct((own.shape[0] * count, 128), own.dtype),
        in_specs=[VMEM],
        out_specs=VMEM,
        compiler_params=params(),
        name="stage",
    )(own)


def join_call(staged, blocks):
    return pl.pallas_call(
        join_kernel,
        out_shape=jax.ShapeDtypeStruct(staged.shape, staged.dtype),
        in_specs=[VMEM] * (1 + len(blocks)),
        out_specs=VMEM,
        input_output_aliases={0: 0},
        compiler_params=params(),
        name="join",
    )(staged, *blocks)


def split3(x):
    high = x.astype(jnp.bfloat16)
    rest = x - high.astype(jnp.float32)
    mid = rest.astype(jnp.bfloat16)
    low = (rest - mid.astype(jnp.float32)).astype(jnp.bfloat16)
    return high.astype(jnp.float32), mid.astype(jnp.float32), low.astype(jnp.float32)


def pack(level, weighted, out_ref):
    mass = weighted[:, 128:]
    out_ref[0:256] = (weighted[:, :128] / mass).astype(jnp.bfloat16)
    rows = jnp.transpose(level + jnp.log2(mass))[0:8]
    left, right = split3(rows[:, :128]), split3(rows[:, 128:])
    at = lax.broadcasted_iota(jnp.int32, (8, 128), 0)
    tile = jnp.where(at == 0, left[0], 0.0)
    for r, part in enumerate((left[1], left[2], right[0], right[1], right[2])):
        tile = jnp.where(at == r + 1, part, tile)
    out_ref[256:272] = jnp.concatenate([tile, tile], axis=0).astype(jnp.bfloat16)


def absorb(level, weighted, part_ref):
    tile = part_ref[256:272].astype(jnp.float32)
    left = tile[0:1] + tile[1:2] + tile[2:3]
    right = tile[3:4] + tile[4:5] + tile[5:6]
    row = jnp.concatenate([left, right], axis=1)
    other = jnp.transpose(jnp.broadcast_to(row, (128, 256)))
    top = jnp.maximum(level, other)
    mine, theirs = jnp.exp2(level - top), jnp.exp2(other - top)
    both = part_ref[0:256].astype(jnp.float32) * theirs
    weighted = jnp.concatenate(
        [weighted[:, :128] * mine + both, weighted[:, 128:] * mine + theirs], axis=1
    )
    return top, weighted


def last_kernel(scale, row, nk, packed, *refs):
    refs = list(refs)
    q_ref, peak_ref, sum_ref = refs[:3]
    pieces, refs = refs[3 : 3 + nk], refs[3 + nk :]
    outs = refs
    queries = blocks_of([q_ref])
    state = [
        (peak_ref[row + at : row + at + ROWS], sum_ref[row + at : row + at + ROWS])
        for at in range(0, 256, ROWS)
    ]
    state = attend(queries, pieces, state, scale)
    level = jnp.concatenate([peak for peak, _ in state], axis=0) * scale
    weighted = jnp.concatenate([total for _, total in state], axis=0)
    if packed:
        pack(level, weighted, outs[0])
    else:
        outs[0][...] = level
        outs[1][...] = weighted


def last_call(query, row, state, pieces, scale, packed=True):
    shapes = jax.ShapeDtypeStruct((272, 128), jnp.bfloat16)
    if not packed:
        shapes = [
            jax.ShapeDtypeStruct((256, 128), jnp.float32),
            jax.ShapeDtypeStruct((256, 256), jnp.float32),
        ]
    return pl.pallas_call(
        functools.partial(last_kernel, scale, row, len(pieces), packed),
        out_shape=shapes,
        in_specs=[VMEM] * (3 + len(pieces)),
        out_specs=VMEM if packed else [VMEM] * 2,
        compiler_params=params(),
        cost_estimate=cost(256, sum(p.shape[0] for p in pieces)),
        name="last_keys",
    )(query, *state, *pieces)


def merge_kernel(q_ref, vw_ref, ow_ref, level_ref, sum_ref, *refs):
    parts, out_ref = refs[:-1], refs[-1]
    level, weighted = level_ref[...], sum_ref[...]
    for part in parts:
        level, weighted = absorb(level, weighted, part)
    mean = (weighted[:, :128] / weighted[:, 128:]).astype(jnp.bfloat16)
    message = jnp.dot(mean, vw_ref[...], preferred_element_type=jnp.float32)
    mixed = q_ref[...].astype(jnp.float32) + jnp.dot(
        message.astype(jnp.bfloat16), ow_ref[...], preferred_element_type=jnp.float32
    )
    out_ref[...] = mixed.astype(jnp.bfloat16)


def merge_call(query, vw, ow, own, parts):
    return pl.pallas_call(
        merge_kernel,
        out_shape=jax.ShapeDtypeStruct((256, 128), jnp.bfloat16),
        in_specs=[VMEM] * (5 + len(parts)),
        out_specs=VMEM,
        compiler_params=params(),
        name="merge",
    )(query, vw, ow, *own, *parts)


def taps_of(row_ref, w_ref, a):
    taps = jnp.concatenate([w_ref[a, b] for b in range(3)], axis=1)
    return jnp.dot(row_ref[...], taps, preferred_element_type=jnp.float32)


def near_rows_kernel(here_ref, sibling_ref, w_ref, bias_ref, out_ref):
    odd = lax.axis_index("ka") % 2
    total = taps_of(here_ref, w_ref, 1) + taps_of(sibling_ref, w_ref, 2 - 2 * odd)
    out_ref[:, 0:128] = total[:, 0:128]
    out_ref[:, 128:256] = total[:, 128:256] + bias_ref[...].astype(jnp.float32)
    out_ref[:, 256:384] = total[:, 256:384]


def refine_kernel(outer_ref, here_ref, near_ref, w_ref, out_ref):
    odd = lax.axis_index("ka") % 2
    total = near_ref[...] + taps_of(outer_ref, w_ref, 2 * odd)
    at = lax.broadcasted_iota(jnp.int32, (256, 128), 0)
    left = jnp.where(at == 0, 0.0, pltpu.roll(total[:, 0:128], 1, 0))
    right = jnp.where(at == 255, 0.0, pltpu.roll(total[:, 256:384], 255, 0))
    conv = left + total[:, 128:256] + right
    out_ref[...] = (here_ref[...].astype(jnp.float32) + jax.nn.gelu(conv)).astype(jnp.bfloat16)


def near_rows_call(here, sibling, w, bias):
    return pl.pallas_call(
        near_rows_kernel,
        out_shape=jax.ShapeDtypeStruct((256, 384), jnp.float32),
        in_specs=[VMEM] * 4,
        out_specs=VMEM,
        compiler_params=params(),
        name="near_rows",
    )(here, sibling, w, bias.reshape(1, 128))


def refine_call(outer, here, near, w):
    return pl.pallas_call(
        refine_kernel,
        out_shape=jax.ShapeDtypeStruct((256, 128), jnp.bfloat16),
        in_specs=[VMEM] * 4,
        out_specs=VMEM,
        compiler_params=params(),
        name="refine",
    )(outer, here, near, w)


def local(feat_first, feat_second, value_weight, out_weight, conv_weight, conv_bias):
    scale = feat_first.shape[1] ** -0.5 * LOG2E
    fence = lax.optimization_barrier
    near = [trade(feat_second, kind, "x", "z") for kind in ("AB", "A", "B")]
    queries = [trade(feat_first, kind, "y") for kind in ("AB", "A", "B")]
    mine = join_call(stage_call(feat_second, 4), near)
    far_a, far_b, far_ab = [trade(mine, kind, "z", "x") for kind in ("A", "B", "AB")]
    twin = swap(mine)
    query_ab, query_a, query_b = queries
    queries = [feat_first, query_a, query_b, query_ab]
    state = keys_call(queries, [mine], scale)
    twin, state = fence((twin, state))
    state = keys_call(queries, [twin], scale, state)
    far_a, far_b, state = fence((far_a, far_b, state))
    twin_a, twin_b = swap(far_a), swap(far_b)
    other = keys_call(queries[1:], [far_a, far_b], scale, state, 256)
    far_ab, other = fence((far_ab, other))
    twin_ab = swap(far_ab)
    away = keys_call(queries[2:], [twin_a, twin_b], scale, other, 256)
    twin_ab, away = fence((twin_ab, away))
    tail = [far_ab, twin_ab]
    from_ab = last_call(query_ab, 256, away, tail, scale)
    from_ab = trade(from_ab, "AB", "y")
    from_b = last_call(query_b, 0, away, tail, scale)
    from_b = trade(from_b, "B", "y")
    from_a = last_call(query_a, 0, other, [twin_a, twin_b] + tail, scale)
    from_a = trade(from_a, "A", "y")
    own = last_call(
        feat_first, 0, state, [far_a, far_b, twin_a, twin_b] + tail, scale, packed=False
    )
    mixed = merge_call(feat_first, value_weight, out_weight, own, (from_ab, from_b, from_a))
    outer = lax.ppermute(mixed, AXES, [(i, i + 1 if i % 2 else i - 1) for i in range(1, 127)])
    sibling = swap(mixed)
    rows = near_rows_call(mixed, sibling, conv_weight, conv_bias)
    refined = refine_call(outer, mixed, rows, conv_weight)
    return refined.reshape(1, 256, 128)


def solution(mesh):
    in_specs = (P(("pb", "ka"), None), P(("ka", "pb"), None), P(), P(), P(), P())
    out_specs = P(("pb", "ka"), None, None)
    return jax.shard_map(local, mesh=mesh, in_specs=in_specs, out_specs=out_specs, check_vma=False)
```

```python
import functools

import jax
import jax.numpy as jnp
from jax import lax
from jax.experimental import pallas as pl
from jax.experimental.pallas import tpu as pltpu
from jax.sharding import PartitionSpec as P


AXES = ("pb", "ka")
SIZES = dict(zh=2, x=4, zl=2, y=4, c=2)
LOG2E = 1.4426950408889634
VMEM = pl.BlockSpec(memory_space=pltpu.VMEM)
NT = (((1,), (1,)), ((), ()))
ROWS = 128
CHUNK = 512


def place(index):
    at = {}
    for name in reversed(SIZES):
        index, at[name] = divmod(index, SIZES[name])
    at["z"] = at["zh"] * 2 + at["zl"]
    return at


def number(at):
    at = dict(at)
    at["zh"], at["zl"] = divmod(at["z"], 2)
    index = 0
    for name, size in SIZES.items():
        index = index * size + at[name]
    return index


def trade(block, kind, *names):
    pairs = []
    for source in range(128):
        at = place(source)
        name = names[at["c"] % len(names)]
        at[name] = dict(A=at[name] ^ 1, B=3 - at[name], AB=at[name] ^ 2)[kind]
        pairs.append((source, number(at)))
    return lax.ppermute(block, AXES, pairs)


def swap(block):
    return lax.ppermute(block, AXES, [(i, i ^ 1) for i in range(128)])


def params():
    return pltpu.CompilerParams(vmem_limit_bytes=48 << 20)


def cost(rows, keys):
    scores = rows * keys
    return pl.CostEstimate(flops=scores * 768, transcendentals=scores, bytes_accessed=1 << 20)


def attend(queries, pieces, state, scale):
    ones = jnp.ones((CHUNK, 128), jnp.bfloat16)
    state = list(state)
    for keys_ref in pieces:
        for at in range(0, keys_ref.shape[0], CHUNK):
            k = keys_ref[at : at + CHUNK]
            v = jnp.concatenate([k, ones], axis=1)
            for b, q in enumerate(queries):
                s = lax.dot_general(q[...], k, NT, preferred_element_type=jnp.float32)
                new = jnp.broadcast_to(jnp.max(s, axis=1, keepdims=True), (ROWS, 128))
                if state[b] is not None:
                    new = jnp.maximum(state[b][0], new)
                all_new = jnp.concatenate([new] * (CHUNK // 128), axis=1)
                p = jnp.exp2(((s - all_new) * scale).astype(jnp.bfloat16))
                weighted = jnp.dot(p, v, preferred_element_type=jnp.float32)
                if state[b] is not None:
                    decay = jnp.exp2((state[b][0] - new) * scale)
                    weighted = state[b][1] * jnp.concatenate([decay, decay], axis=1) + weighted
                state[b] = (new, weighted)
    return state


def blocks_of(refs):
    return [ref.at[pl.ds(at, ROWS)] for ref in refs for at in range(0, ref.shape[0], ROWS)]


def keys_kernel(scale, nq, nk, started, row, *refs):
    refs = list(refs)
    take = lambda n: [refs.pop(0) for _ in range(n)]
    queries, pieces = blocks_of(take(nq)), take(nk)
    state = [None] * len(queries)
    if started:
        peaks, sums = blocks_of(take(1)), blocks_of(take(1))
        first = row // ROWS
        state = [(peaks[first + b][...], sums[first + b][...]) for b in range(len(queries))]
    peaks, sums = blocks_of(refs[:1]), blocks_of(refs[1:])
    for b, (peak, weighted) in enumerate(attend(queries, pieces, state, scale)):
        peaks[b][...] = peak
        sums[b][...] = weighted


def keys_call(queries, pieces, scale, state=(), row=0):
    rows = sum(q.shape[0] for q in queries)
    return pl.pallas_call(
        functools.partial(keys_kernel, scale, len(queries), len(pieces), bool(state), row),
        out_shape=[
            jax.ShapeDtypeStruct((rows, 128), jnp.float32),
            jax.ShapeDtypeStruct((rows, 256), jnp.float32),
        ],
        in_specs=[VMEM] * (len(queries) + len(pieces) + len(state)),
        out_specs=[VMEM] * 2,
        compiler_params=params(),
        cost_estimate=cost(rows, sum(p.shape[0] for p in pieces)),
        name="keys",
    )(*queries, *pieces, *state)


def pause_kernel(out_ref):
    out_ref[...] = jnp.zeros_like(out_ref)


def pause_call():
    return pl.pallas_call(
        pause_kernel,
        out_shape=jax.ShapeDtypeStruct((8, 128), jnp.float32),
        out_specs=VMEM,
        compiler_params=params(),
        cost_estimate=pl.CostEstimate(flops=20_000_000_000, transcendentals=0, bytes_accessed=4096),
        name="pause",
    )()


def join_kernel(*refs):
    blocks, out_ref = refs[:-2], refs[-1]
    for i, ref in enumerate(blocks):
        rows = ref.shape[0]
        out_ref[i * rows : (i + 1) * rows] = ref[...]


def join_call(blocks, after):
    rows = sum(block.shape[0] for block in blocks)
    return pl.pallas_call(
        join_kernel,
        out_shape=jax.ShapeDtypeStruct((rows, 128), blocks[0].dtype),
        in_specs=[VMEM] * (len(blocks) + 1),
        out_specs=VMEM,
        compiler_params=params(),
        name="join",
    )(*blocks, after)


def split3(x):
    high = x.astype(jnp.bfloat16)
    rest = x - high.astype(jnp.float32)
    mid = rest.astype(jnp.bfloat16)
    low = (rest - mid.astype(jnp.float32)).astype(jnp.bfloat16)
    return high.astype(jnp.float32), mid.astype(jnp.float32), low.astype(jnp.float32)


def pack(level, weighted, out_ref):
    mass = weighted[:, 128:]
    out_ref[0:256] = (weighted[:, :128] / mass).astype(jnp.bfloat16)
    rows = jnp.transpose(level + jnp.log2(mass))[0:8]
    left, right = split3(rows[:, :128]), split3(rows[:, 128:])
    at = lax.broadcasted_iota(jnp.int32, (8, 128), 0)
    tile = jnp.where(at == 0, left[0], 0.0)
    for r, part in enumerate((left[1], left[2], right[0], right[1], right[2])):
        tile = jnp.where(at == r + 1, part, tile)
    out_ref[256:272] = jnp.concatenate([tile, tile], axis=0).astype(jnp.bfloat16)


def absorb(level, weighted, part_ref):
    tile = part_ref[256:272].astype(jnp.float32)
    left = tile[0:1] + tile[1:2] + tile[2:3]
    right = tile[3:4] + tile[4:5] + tile[5:6]
    row = jnp.concatenate([left, right], axis=1)
    other = jnp.transpose(jnp.broadcast_to(row, (128, 256)))
    top = jnp.maximum(level, other)
    mine, theirs = jnp.exp2(level - top), jnp.exp2(other - top)
    both = part_ref[0:256].astype(jnp.float32) * theirs
    weighted = jnp.concatenate(
        [weighted[:, :128] * mine + both, weighted[:, 128:] * mine + theirs], axis=1
    )
    return top, weighted


def last_kernel(scale, row, nk, packed, *refs):
    refs = list(refs)
    q_ref, peak_ref, sum_ref = refs[:3]
    pieces, refs = refs[3 : 3 + nk], refs[3 + nk :]
    outs = refs
    queries = blocks_of([q_ref])
    state = [
        (peak_ref[row + at : row + at + ROWS], sum_ref[row + at : row + at + ROWS])
        for at in range(0, 256, ROWS)
    ]
    state = attend(queries, pieces, state, scale)
    level = jnp.concatenate([peak for peak, _ in state], axis=0) * scale
    weighted = jnp.concatenate([total for _, total in state], axis=0)
    if packed:
        pack(level, weighted, outs[0])
    else:
        outs[0][...] = level
        outs[1][...] = weighted


def last_call(query, row, state, pieces, scale, packed=True):
    shapes = jax.ShapeDtypeStruct((272, 128), jnp.bfloat16)
    if not packed:
        shapes = [
            jax.ShapeDtypeStruct((256, 128), jnp.float32),
            jax.ShapeDtypeStruct((256, 256), jnp.float32),
        ]
    return pl.pallas_call(
        functools.partial(last_kernel, scale, row, len(pieces), packed),
        out_shape=shapes,
        in_specs=[VMEM] * (3 + len(pieces)),
        out_specs=VMEM if packed else [VMEM] * 2,
        compiler_params=params(),
        cost_estimate=cost(256, sum(p.shape[0] for p in pieces)),
        name="last_keys",
    )(query, *state, *pieces)


def merge_kernel(q_ref, vw_ref, ow_ref, level_ref, sum_ref, *refs):
    parts, out_ref = refs[:-1], refs[-1]
    level, weighted = level_ref[...], sum_ref[...]
    for part in parts:
        level, weighted = absorb(level, weighted, part)
    mean = (weighted[:, :128] / weighted[:, 128:]).astype(jnp.bfloat16)
    message = jnp.dot(mean, vw_ref[...], preferred_element_type=jnp.float32)
    mixed = q_ref[...].astype(jnp.float32) + jnp.dot(
        message.astype(jnp.bfloat16), ow_ref[...], preferred_element_type=jnp.float32
    )
    out_ref[...] = mixed.astype(jnp.bfloat16)


def merge_call(query, vw, ow, own, parts):
    return pl.pallas_call(
        merge_kernel,
        out_shape=jax.ShapeDtypeStruct((256, 128), jnp.bfloat16),
        in_specs=[VMEM] * (5 + len(parts)),
        out_specs=VMEM,
        compiler_params=params(),
        name="merge",
    )(query, vw, ow, *own, *parts)


def taps_of(row_ref, w_ref, a):
    taps = jnp.concatenate([w_ref[a, b] for b in range(3)], axis=1)
    return jnp.dot(row_ref[...], taps, preferred_element_type=jnp.float32)


def near_rows_kernel(here_ref, sibling_ref, w_ref, bias_ref, out_ref):
    odd = lax.axis_index("ka") % 2
    total = taps_of(here_ref, w_ref, 1) + taps_of(sibling_ref, w_ref, 2 - 2 * odd)
    out_ref[:, 0:128] = total[:, 0:128]
    out_ref[:, 128:256] = total[:, 128:256] + bias_ref[...].astype(jnp.float32)
    out_ref[:, 256:384] = total[:, 256:384]


def refine_kernel(outer_ref, here_ref, near_ref, w_ref, out_ref):
    odd = lax.axis_index("ka") % 2
    total = near_ref[...] + taps_of(outer_ref, w_ref, 2 * odd)
    at = lax.broadcasted_iota(jnp.int32, (256, 128), 0)
    left = jnp.where(at == 0, 0.0, pltpu.roll(total[:, 0:128], 1, 0))
    right = jnp.where(at == 255, 0.0, pltpu.roll(total[:, 256:384], 255, 0))
    conv = left + total[:, 128:256] + right
    out_ref[...] = (here_ref[...].astype(jnp.float32) + jax.nn.gelu(conv)).astype(jnp.bfloat16)


def near_rows_call(here, sibling, w, bias):
    return pl.pallas_call(
        near_rows_kernel,
        out_shape=jax.ShapeDtypeStruct((256, 384), jnp.float32),
        in_specs=[VMEM] * 4,
        out_specs=VMEM,
        compiler_params=params(),
        name="near_rows",
    )(here, sibling, w, bias.reshape(1, 128))


def refine_call(outer, here, near, w):
    return pl.pallas_call(
        refine_kernel,
        out_shape=jax.ShapeDtypeStruct((256, 128), jnp.bfloat16),
        in_specs=[VMEM] * 4,
        out_specs=VMEM,
        compiler_params=params(),
        name="refine",
    )(outer, here, near, w)


def local(feat_first, feat_second, value_weight, out_weight, conv_weight, conv_bias):
    scale = feat_first.shape[1] ** -0.5 * LOG2E
    fence = lax.optimization_barrier
    near = [trade(feat_second, kind, "x", "z") for kind in ("AB", "A", "B")]
    queries = [trade(feat_first, kind, "y") for kind in ("AB", "A", "B")]
    mine = join_call([feat_second] + near, pause_call())
    far_a, far_b, far_ab = [trade(mine, kind, "z", "x") for kind in ("A", "B", "AB")]
    twin = swap(mine)
    query_ab, query_a, query_b = queries
    queries = [feat_first, query_a, query_b, query_ab]
    state = keys_call(queries, [mine], scale)
    twin, state = fence((twin, state))
    state = keys_call(queries, [twin], scale, state)
    far_a, far_b, state = fence((far_a, far_b, state))
    twin_a, twin_b = swap(far_a), swap(far_b)
    other = keys_call(queries[1:], [far_a, far_b], scale, state, 256)
    far_ab, other = fence((far_ab, other))
    twin_ab = swap(far_ab)
    away = keys_call(queries[2:], [twin_a, twin_b], scale, other, 256)
    twin_ab, away = fence((twin_ab, away))
    tail = [far_ab, twin_ab]
    from_ab = last_call(query_ab, 256, away, tail, scale)
    from_ab = trade(from_ab, "AB", "y")
    from_b = last_call(query_b, 0, away, tail, scale)
    from_b = trade(from_b, "B", "y")
    from_a = last_call(query_a, 0, other, [twin_a, twin_b] + tail, scale)
    from_a = trade(from_a, "A", "y")
    own = last_call(
        feat_first, 0, state, [far_a, far_b, twin_a, twin_b] + tail, scale, packed=False
    )
    mixed = merge_call(feat_first, value_weight, out_weight, own, (from_ab, from_b, from_a))
    outer = lax.ppermute(mixed, AXES, [(i, i + 1 if i % 2 else i - 1) for i in range(1, 127)])
    sibling = swap(mixed)
    rows = near_rows_call(mixed, sibling, conv_weight, conv_bias)
    refined = refine_call(outer, mixed, rows, conv_weight)
    return refined.reshape(1, 256, 128)


def solution(mesh):
    in_specs = (P(("pb", "ka"), None), P(("ka", "pb"), None), P(), P(), P(), P())
    out_specs = P(("pb", "ka"), None, None)
    return jax.shard_map(local, mesh=mesh, in_specs=in_specs, out_specs=out_specs, check_vma=False)
```
